32 devices in a mesh: slab: 4 (over y, x), block: 8 (over z, core).
Axes of the slice: x: 2, y: 2, z: 4, core: 2. Of those that a mesh axis runs over, the one named last changes fastest.
Arguments:
- lanczos_vector: float32 [3, 32, 64, 256], P(None, 'slab', 'block'), may hold values from -200 to 200
- previous_vector: float32 [3, 32, 64, 256], P(None, 'slab', 'block'), may hold values from -30 to 30
- previous_beta: float32 [], replicated, may hold values from 0.3 to 1
- locked_vectors: float32 [16, 3, 32, 64, 256], P(None, None, 'slab', 'block'), may hold values from -0.0039867997 to 0.0039867997
- occupancy: int32 [4, 8, 32], P('slab', 'block'), may hold values 0 or 1
- young: float32 [32, 64, 256], P('slab', 'block'), may hold values from 0.5 to 4
- couplings: float32 [13, 3, 3], replicated, may hold values from -1 to 1, as said below
- coarse_inverse: float32 [96, 96], P(('slab', 'block')), may hold values from -45 to 165, as said below
Outputs:
- remainder: float32 [3, 32, 64, 256], P(None, 'slab', 'block')
- coefficients: float32 [2], replicated
- projections: float32 [16], replicated
The draws below stay inside these ranges and needn't reach their ends.
Inputs may be any that keep to these rules, and one draw needn't show every extreme that they name: `couplings`: each block is symmetric and positive definite, with positive diagonal larger than the sum of its off-diagonal magnitudes. `coarse_inverse`: symmetric and positive definite.
All inputs are finite; a program needn't handle non-finite values. No bound on the sum of `occupancy` on one device may be relied on, other than what follows from the above.
Results may differ from the reference program's by a relative error of at most 0.0003.
Values sent between devices are 32-bit elements; how exact they have to be, the bound alone decides.
No kernel may reach another device: no remote copies, remote signals or barrier semaphores. Data moves between devices by JAX's collectives and lax.ppermute only.
A program may use at most 128 MiB of HBM per device.

```python
import math
import jax
import jax.numpy as jnp
from jax import lax

LOCKED = 16
CX = 8
CY = 8
BRICK = 8
ITERS = 3
NX = 32
NY = 64
NZ = 256
NCOARSE = 96
N_SLAB = 4
N_BLOCK = 8


def locked_core(key):
    core_key = jax.random.fold_in(key, 11)
    values = jnp.clip(jax.random.normal(core_key, (LOCKED, 3, NX, NY, NZ)), -5.0, 5.0)
    return values.astype(jnp.float32)


def locked_weights(key):
    weight_key = jax.random.fold_in(key, 23)
    sign_key, size_key = jax.random.split(weight_key)
    signs = jax.random.randint(sign_key, (LOCKED,), 0, 2).astype(jnp.float32) * 2.0 - 1.0
    sizes = jax.random.uniform(size_key, (LOCKED,), minval=0.1, maxval=0.3)
    return signs * sizes


def draw_locked_vectors(key, part):
    scale_factor = (3.0 * NX * NY * NZ) ** (-0.5)
    return (locked_core(key) * scale_factor).astype(jnp.float32)


def draw_previous_vector(key, part):
    noise_key = jax.random.fold_in(key, 37)
    noise_part = jnp.clip(jax.random.normal(noise_key, (3, NX, NY, NZ)), -6.0, 6.0)
    core = locked_core(key)
    weights = locked_weights(key)
    values = noise_part
    for index in range(LOCKED):
        values = values + weights[index] * core[index]
    return values.astype(jnp.float32)


def draw_lanczos_vector(key, part):
    first_key = jax.random.fold_in(key, 0)
    along_x = jnp.arange(NX, dtype=jnp.float32) / NX
    along_y = jnp.arange(NY, dtype=jnp.float32) / NY
    rising = (3.0 ** along_x)[:, None, None] * (3.0 ** along_y)[None, :, None]
    values = jnp.clip(jax.random.normal(first_key, (3, NX, NY, NZ)), -5.5, 5.5) * rising[None]
    return values.astype(jnp.float32)


def draw_couplings(key, part):
    diag_key, off_key = jax.random.split(key)
    diag_part = jax.random.uniform(diag_key, (13, 3), minval=0.5, maxval=1.5)
    raw_values = jax.random.uniform(off_key, (13, 3, 3), minval=-0.2, maxval=0.2)
    upper_mask = jnp.triu(jnp.ones((3, 3), jnp.float32), 1)
    offdiag = raw_values * upper_mask[None]
    offdiag = offdiag + jnp.swapaxes(offdiag, 1, 2)
    blocks = offdiag + diag_part[:, :, None] * jnp.eye(3, dtype=jnp.float32)[None]
    return (blocks / 13.0).astype(jnp.float32)


def draw_coarse_inverse(key, part):
    diag_key, off_key = jax.random.split(key)
    pair_key = jax.random.fold_in(key, 53)
    sign_key, size_key = jax.random.split(pair_key)
    raw_values = jax.random.uniform(off_key, (NCOARSE, NCOARSE), minval=-1.0, maxval=1.0) / NCOARSE
    half_count = NCOARSE // 2
    rows = jnp.arange(NCOARSE, dtype=jnp.int32)
    partner = (rows + half_count) % NCOARSE
    is_pair = (rows[None, :] == partner[:, None]).astype(jnp.float32)
    base_index = rows % half_count
    signs = jax.random.randint(sign_key, (half_count,), 0, 2).astype(jnp.float32) * 2.0 - 1.0
    sizes = jax.random.uniform(size_key, (half_count,), minval=0.5, maxval=1.0)
    pair_values = (signs * sizes)[base_index]
    symmetric = jnp.triu(raw_values, 1)
    symmetric = symmetric + symmetric.T
    symmetric = symmetric * (1.0 - is_pair) + is_pair * pair_values[:, None]
    diag_part = jax.random.uniform(diag_key, (NCOARSE,), minval=2.5, maxval=4.0)
    return (40.0 * (symmetric + jnp.diag(diag_part))).astype(jnp.float32)


def place_ends(values, stream_key, low, top_value):
    longest = values.shape.index(max(values.shape))
    spots = []
    for shift in (0, 1):
        where = [jax.random.randint(jax.random.fold_in(stream_key, axis), (), 0, length) for axis, length in enumerate(values.shape)]
        where[longest] = (where[longest] + shift) % values.shape[longest]
        spots.append(tuple(where))
    return values.at[spots[0]].set(low).at[spots[1]].set(top_value)


def block_scale(stream_key, shape, shards, smallest, high):
    def one(dim, blocks):
        heights = jax.random.uniform(jax.random.fold_in(jax.random.fold_in(stream_key, 6), dim), (blocks,), jnp.float32, smallest / len(shards), high / len(shards))
        return jnp.repeat(jnp.exp(heights), shape[dim] // blocks).reshape((-1,) + (1,) * (len(shape) - dim - 1))

    loudness = one(*shards[0])
    for cut in shards[1:]:
        loudness = loudness * one(*cut)
    return loudness


def setup_inputs(seed: int = 0) -> dict:
    key_of = jax.random.split(jax.random.key(seed), 9)
    lanczos_vector = draw_lanczos_vector(jax.random.fold_in(key_of[8], 71), 0)
    previous_vector = draw_previous_vector(jax.random.fold_in(key_of[8], 71), 0)
    previous_beta = jnp.clip(jax.random.uniform(key_of[2], (), jnp.float32, 0.3, 1.0), 0.3, 1.0)
    locked_vectors = draw_locked_vectors(jax.random.fold_in(key_of[8], 71), 0)
    occupancy = place_ends((jax.random.randint(key_of[4], (NX // BRICK, NY // BRICK, NZ // BRICK), 0, 5) < 3).astype(jnp.int32), jax.random.fold_in(key_of[4], 1), 0, 1)
    young = jnp.clip(jnp.exp(math.log(4.0) - 2.0794415 * jax.random.uniform(key_of[5], (NX, NY, NZ), jnp.float32) ** block_scale(key_of[5], (NX, NY, NZ), ((0, 4), (1, 8)), -0.2, 0.2)), 0.5, 4.0)
    couplings = draw_couplings(jax.random.fold_in(key_of[8], 71), 0)
    coarse_inverse = draw_coarse_inverse(jax.random.fold_in(key_of[8], 71), 0)
    return {"lanczos_vector": lanczos_vector, "previous_vector": previous_vector, "previous_beta": previous_beta, "locked_vectors": locked_vectors, "occupancy": occupancy, "young": young, "couplings": couplings, "coarse_inverse": coarse_inverse}


SHIFT_MASS = 0.02
SMOOTH_WEIGHT = 0.5
VOID_DENSITY = 0.1
HIGHEST_PRECISION = lax.Precision.HIGHEST

def offset_list():
    offsets = []
    for step_x in (-1, 0, 1):
        for step_y in (-1, 0, 1):
            for step_z in (-1, 0, 1):
                offsets.append((step_x, step_y, step_z))
    return offsets

def pair_block(couplings, number):
    if number < 13:
        return couplings[number]
    return couplings[26 - number]

def operate_padded(vector_field, padded_weighted, padded_root, stiffness, root_stiff, couplings):
    span_x, span_y, span_z = (vector_field.shape[1], vector_field.shape[2], vector_field.shape[3])
    accumulate = jnp.zeros_like(vector_field)
    for number, (step_x, step_y, step_z) in enumerate(offset_list()):
        if number == 13:
            continue
        matrix_pair = pair_block(couplings, number)
        root_near = padded_root[1 + step_x:1 + step_x + span_x, 1 + step_y:1 + step_y + span_y, 1 + step_z:1 + step_z + span_z]
        weighted_near = padded_weighted[:, 1 + step_x:1 + step_x + span_x, 1 + step_y:1 + step_y + span_y, 1 + step_z:1 + step_z + span_z]
        differ = root_near[None] * vector_field - weighted_near
        for column in range(3):
            accumulate = accumulate + matrix_pair[:, column][:, None, None, None] * differ[column][None]
    return SHIFT_MASS * stiffness[None] * vector_field + root_stiff[None] * accumulate

def diagonal_of(padded_root, stiffness, root_stiff, couplings):
    span_x, span_y, span_z = stiffness.shape
    accumulate = jnp.zeros((3, span_x, span_y, span_z), jnp.float32)
    for number, (step_x, step_y, step_z) in enumerate(offset_list()):
        if number == 13:
            continue
        matrix_pair = pair_block(couplings, number)
        root_near = padded_root[1 + step_x:1 + step_x + span_x, 1 + step_y:1 + step_y + span_y, 1 + step_z:1 + step_z + span_z]
        accumulate = accumulate + jnp.diagonal(matrix_pair)[:, None, None, None] * root_near[None]
    return SHIFT_MASS * stiffness[None] + root_stiff[None] * accumulate

def reference(lanczos_vector, previous_vector, previous_beta, locked_vectors, occupancy, young, couplings, coarse_inverse):
    density = jnp.where(occupancy == 1, 1.0, VOID_DENSITY).astype(jnp.float32)
    density = jnp.repeat(jnp.repeat(jnp.repeat(density, BRICK, 0), BRICK, 1), BRICK, 2)
    stiffness = density * young
    root_stiff = jnp.sqrt(stiffness)
    padded_root = jnp.pad(root_stiff, 1)
    diagonal = diagonal_of(padded_root, stiffness, root_stiff, couplings)

    def operate(vector_field):
        padded_weighted = jnp.pad(root_stiff[None] * vector_field, ((0, 0), (1, 1), (1, 1), (1, 1)))
        return operate_padded(vector_field, padded_weighted, padded_root, stiffness, root_stiff, couplings)

    def coarse(vector_field):
        block_means = lax.optimization_barrier(jnp.mean(vector_field.reshape(3, N_SLAB, CX, N_BLOCK, CY, NZ), axis=(2, 4, 5)))
        gathered = jnp.transpose(block_means, (1, 2, 0)).reshape(NCOARSE)
        coarse_values = jnp.dot(coarse_inverse, gathered, precision=HIGHEST_PRECISION)
        spread = jnp.transpose(coarse_values.reshape(N_SLAB, N_BLOCK, 3), (2, 0, 1))
        spread = jnp.repeat(jnp.repeat(spread, CX, 1), CY, 2)
        return jnp.broadcast_to(spread[:, :, :, None], vector_field.shape)

    def precondition(residual):
        smooth_first = SMOOTH_WEIGHT * residual / diagonal
        remain = residual - operate(smooth_first)
        second = smooth_first + coarse(remain)
        return second + SMOOTH_WEIGHT * (residual - operate(second)) / diagonal
    solution = jnp.zeros_like(lanczos_vector)
    residual = lanczos_vector
    smoothed = precondition(residual)
    direction = smoothed
    gamma_now = jnp.sum(residual * smoothed)
    for number in range(ITERS):
        mapped = operate(direction)
        step_size = gamma_now / jnp.sum(direction * mapped)
        solution = solution + step_size * direction
        residual = residual - step_size * mapped
        if number + 1 < ITERS:
            smoothed = precondition(residual)
            gamma_next = jnp.sum(residual * smoothed)
            direction = smoothed + gamma_next / gamma_now * direction
            gamma_now = gamma_next
    alpha_now = jnp.sum(lanczos_vector * solution) / jnp.sum(lanczos_vector * lanczos_vector)
    lanczos_part = solution - alpha_now * lanczos_vector - previous_beta * previous_vector
    projections = jnp.einsum('kcxyz,cxyz->k', locked_vectors, lanczos_part, precision=HIGHEST_PRECISION)
    remainder = lanczos_part - jnp.einsum('kcxyz,k->cxyz', locked_vectors, projections, precision=HIGHEST_PRECISION)
    cell_count = 3.0 * NX * NY * NZ
    beta_norm = jnp.sqrt(jnp.sum(remainder * remainder) / cell_count)
    return (remainder, jnp.stack([alpha_now, beta_norm]), projections)
```

```python
import functools

import jax
import jax.numpy as jnp
from jax import lax
from jax.experimental import pallas as pl
from jax.experimental.pallas import tpu as pltpu
from jax.sharding import PartitionSpec as P

BRICK = 8
ITERS = 3
SHIFT_MASS = 0.02
SMOOTH_WEIGHT = 0.5
VOID_DENSITY = 0.1

AXES = ("slab", "block")
LANES = 128
WIDE = (8, 24)
MID = (4, 16)
OWN = (0, 8)
REACH = 2 * ITERS
PAIRS = [(n // 9 - 1, n // 3 % 3 - 1, n % 3 - 1) for n in range(13)]
SYM = [(0, 0), (0, 1), (0, 2), (1, 1), (1, 2), (2, 2)]
SLOT = {}
for number, (first, second) in enumerate(SYM):
    SLOT[first, second] = number
    SLOT[second, first] = number

f32 = jnp.float32


def shift_store(dest, at, fields, source, target):
    src_off, src_rows = source
    dst_off, dst_rows = target
    depth = fields[0].shape[1]
    lane = lax.broadcasted_iota(jnp.int32, (dst_rows, depth), 1)
    for comp, field in enumerate(fields):
        for dy in (-1, 0, 1):
            shift = src_off - dst_off + dy
            moved = field if shift == 0 else pltpu.roll(field, (-shift) % src_rows, 0)
            if dst_rows != src_rows:
                moved = moved[:dst_rows]
            for dz in (-1, 0, 1):
                if dz == 0:
                    out = moved
                else:
                    edge = 0 if dz < 0 else depth - 1
                    out = jnp.where(lane == edge, 0.0, pltpu.roll(moved, (-dz) % depth, 1))
                dest[((dy + 1) * 3 + dz + 1) * len(fields) + comp, at] = out


def pair_slots(pair):
    dx, dy, dz = pair
    return dx, (dy + 1) * 3 + dz + 1, (1 - dy) * 3 + 1 - dz


def stencil(moved, at, coup, diag):
    total = [None] * 3
    for number, pair in enumerate(PAIRS):
        dx, plus, minus = pair_slots(pair)
        sums = [moved[plus * 3 + c, at + dx] + moved[minus * 3 + c, at - dx] for c in range(3)]
        for k in range(3):
            for c in range(3):
                term = coup[number * 9 + k * 3 + c] * sums[c]
                total[k] = term if total[k] is None else total[k] + term
    near = [moved[4 * 3 + c, at] for c in range(3)]
    out = []
    for k in range(3):
        acc = diag(SLOT[k, 0]) * near[0] + diag(SLOT[k, 1]) * near[1]
        acc = acc + diag(SLOT[k, 2]) * near[2]
        out.append(acc - total[k])
    return out, near


def loop(low, high, body):
    def step(i, carry):
        body(i)
        return carry

    lax.fori_loop(low, high, step, 0)


def row_sum(x):
    return jnp.sum(x, axis=0, keepdims=True)


def to_lanes(rows):
    column = jnp.sum(rows, axis=1, keepdims=True)
    count = rows.shape[0]
    here = lax.broadcasted_iota(jnp.int32, (count, LANES), 0)
    lane = lax.broadcasted_iota(jnp.int32, (count, LANES), 1)
    return row_sum(jnp.where(here == lane, column, 0.0))


def pick(row, index):
    lane = lax.broadcasted_iota(jnp.int32, row.shape, 1)
    return jnp.sum(jnp.where(lane == index, row, 0.0), axis=1, keepdims=True)


def scalar(one):
    return one[0, 0]


def coarse_values(means, rows_of, where, counts, store):
    total = None
    for k in range(3):
        part = row_sum(rows_of(k) * means[:, k : k + 1])
        total = part if total is None else total + part
    for bx in range(3):
        for by in range(3):
            spot = (where[0] + bx - 1) * counts[1] + where[1] + by - 1
            for k in range(3):
                store[(bx * 3 + by) * 3 + k] = scalar(pick(total, spot * 3 + k))


def correction(store, x, k, layout, span, depth):
    off, rows = layout
    base = lax.div(x + span, span) * 9 + k
    row = lax.broadcasted_iota(jnp.int32, (rows, depth), 0)
    high = jnp.where(row < off + 8, store[base + 3], store[base + 6])
    return jnp.where(row < off, store[base], high)


def send_row(row, count):
    return jnp.broadcast_to(row, (count, row.shape[1]))


def setup_kernel(
    dims, where, coup, even, odd, mid, cinv,
    kh_w, h_w, v_w, root_w, kh_m, h_m, v_m, root_m, msg,
    moved_root, root_all, moved_own, sums,
):
    span, depth, devices = dims
    halo = REACH + 1
    flip = where[1] % 2 == 1

    def wide(comp, x):
        first, second = even[comp, x], odd[comp, x]
        low = jnp.where(flip, first, second)
        high = jnp.where(flip, second, first)
        return jnp.concatenate([low, mid[comp, x], high], axis=0)

    def roots(x):
        root = jnp.sqrt(wide(3, x))
        root_all[x] = root
        shift_store(moved_root, x, [root], WIDE, WIDE)

    loop(0, span + 2 * halo, roots)

    def repack(field):
        return pltpu.roll(field, WIDE[1] - (WIDE[0] - MID[0]), 0)[: MID[1]]

    def diagonals(x, also_mid):
        at = x + 1
        total = [None] * 6
        for number, pair in enumerate(PAIRS):
            dx, plus, minus = pair_slots(pair)
            both = moved_root[plus, at + dx] + moved_root[minus, at - dx]
            for slot, (k, c) in enumerate(SYM):
                term = coup[number * 9 + k * 3 + c] * both
                total[slot] = term if total[slot] is None else total[slot] + term
        root = root_all[at]
        inside = root > 0.0
        inverse = jnp.where(inside, 1.0 / jnp.where(inside, root, 1.0), 0.0)
        root_w[x] = root
        m = x - (REACH - 4)
        if also_mid:
            root_m[m] = repack(root)
        for slot, (k, c) in enumerate(SYM):
            value = total[slot] * inverse
            if k == c:
                value = value + SHIFT_MASS
                half = jnp.where(inside, SMOOTH_WEIGHT / value, 0.0)
                h_w[k, x] = half
                vector = wide(k, at) * inverse
                v_w[k, x] = vector
                if also_mid:
                    h_m[k, m] = repack(half)
                    v_m[k, m] = repack(vector)
            kh_w[slot, x] = value
            if also_mid:
                kh_m[slot, m] = repack(value)

    edge = REACH - 4
    loop(0, edge, lambda x: diagonals(x, False))
    loop(edge, edge + span + 8, lambda x: diagonals(x, True))
    loop(edge + span + 8, span + 2 * REACH, lambda x: diagonals(x, False))

    def smooth(x):
        at = x + REACH - 1
        shift_store(moved_own, x, [h_w[k, at] * v_w[k, at] for k in range(3)], WIDE, OWN)

    loop(0, span + 2, smooth)

    def remain(x, carry):
        at = x + REACH
        own = slice(WIDE[0], WIDE[0] + 8)
        image, _ = stencil(moved_own, x + 1, coup, lambda slot: kh_w[slot, at, own])
        return tuple(carry[k] + root_w[at, own] * (v_w[k, at, own] - image[k]) for k in range(3))

    zero = jnp.zeros((8, depth), f32)
    parts = lax.fori_loop(0, span, remain, (zero, zero, zero))
    sums[...] = jnp.zeros_like(sums)
    for k in range(3):
        sums[k : k + 1] = row_sum(parts[k])
    row = to_lanes(sums[...]) * (1.0 / (span * 8 * depth))
    msg[:, :LANES] = send_row(row, devices)
    width = cinv.shape[1]
    padded = (msg.shape[1] - LANES) // 3
    for k in range(3):
        low = LANES + k * padded
        if padded != width:
            msg[:, low : low + padded] = jnp.zeros((devices, padded), f32)
        msg[:, low : low + width] = jnp.broadcast_to(cinv[k : k + 1], (devices, width))


def iterate(dims, level, layouts, coup, store, residual, half, root, diag, moved, moved_next, own_z):
    span, depth = dims
    source, first, second = layouts

    def begin(x):
        fields = []
        for k in range(3):
            fix = correction(store, x - level, k, source, span, depth)
            fields.append(half(k, x) * residual(k, x) + root(x) * fix)
        shift_store(moved, x, fields, source, first)

    loop(0, span + 2 * level, begin)

    def middle(x):
        at = x + 1
        image, near = stencil(moved, at, coup, diag[0](at))
        fields = [near[k] + half(k, at) * (residual(k, at) - image[k]) for k in range(3)]
        own_z(x, fields)
        shift_store(moved_next, x, fields, first, second)

    loop(0, span + 2 * level - 2, middle)


def own_rows(layout):
    return slice(layout[0], layout[0] + 8)


def means_of(dims, coup, root, half, mapped, diag, moved_own):
    span, depth = dims

    def begin(x):
        shift_store(moved_own, x, [half(k, x) * mapped(k, x) for k in range(3)], MID, OWN)

    loop(0, span + 2, begin)

    def body(x, carry):
        image, _ = stencil(moved_own, x + 1, coup, lambda slot: diag(slot, x))
        return tuple(carry[k] + root(x) * (mapped_own(k, x) - image[k]) for k in range(3))

    def mapped_own(k, x):
        return pltpu.roll(mapped(k, x + 1), MID[1] - MID[0], 0)[:8]

    zero = jnp.zeros((8, depth), f32)
    return lax.fori_loop(0, span, body, (zero, zero, zero))


def own_of(field):
    return pltpu.roll(field, MID[1] - MID[0], 0)[:8]


def first_kernel(
    dims, counts, where, coup, got, kh_w, h_w, v_w, root_w, kh_m, h_m,
    z_own, mapped, msg,
    moved, moved_next, moved_own, store, sums,
):
    span, depth, devices = dims
    level = REACH
    padded = (got.shape[1] - LANES) // 3
    coarse_values(
        got[:, :LANES],
        lambda k: got[:, LANES + k * padded : LANES + (k + 1) * padded],
        where, counts, store,
    )

    def keep(x, fields):
        at = x - (level - 1)

        @pl.when((at >= 0) & (at < span))
        def _():
            for k in range(3):
                z_own[k, at] = fields[k][own_rows(WIDE)]

    iterate(
        (span, depth), level, (WIDE, WIDE, MID), coup, store,
        lambda k, x: v_w[k, x], lambda k, x: h_w[k, x], lambda x: root_w[x],
        (lambda at: lambda slot: kh_w[slot, at],), moved, moved_next, keep,
    )

    def image(x):
        out, _ = stencil(moved_next, x + 1, coup, lambda slot: kh_m[slot, x])
        for k in range(3):
            mapped[k, x] = out[k]

    loop(0, span + 2 * level - 4, image)
    inner = level - 2
    parts = means_of(
        (span, depth), coup,
        lambda x: root_w[x + REACH, own_rows(WIDE)],
        lambda k, x: h_m[k, x + 3], lambda k, x: mapped[k, x + inner - 1],
        lambda slot, x: kh_w[slot, x + REACH, own_rows(WIDE)], moved_own,
    )

    def dots(x, carry):
        gamma, delta = carry
        for k in range(3):
            z = z_own[k, x]
            gamma = gamma + v_w[k, x + REACH, own_rows(WIDE)] * z
            delta = delta + own_of(mapped[k, x + inner]) * z
        return gamma, delta

    zero = jnp.zeros((8, depth), f32)
    gamma, delta = lax.fori_loop(0, span, dots, (zero, zero))
    scale = 1.0 / (span * 8 * depth)
    sums[...] = jnp.zeros_like(sums)
    for k in range(3):
        sums[k : k + 1] = row_sum(parts[k]) * scale
    sums[3:4] = row_sum(gamma)
    sums[4:5] = row_sum(delta)
    msg[...] = send_row(to_lanes(sums[...]), devices)


def second_kernel(
    dims, counts, where, coup, got, first, kh_m, h_m, v_m, root_m, kh_w, z_old, mapped_old,
    z_own, mapped, residual, means, msg,
    moved, moved_next, moved_own, store, sums,
):
    span, depth, devices = dims
    level = REACH - 2
    total = row_sum(got[...])
    gamma = pick(total, 3)
    step = gamma / pick(total, 4)
    padded = (first.shape[1] - LANES) // 3
    means[...] = first[:, :LANES] - step * got[...]
    coarse_values(
        means[...],
        lambda k: first[:, LANES + k * padded : LANES + (k + 1) * padded],
        where, counts, store,
    )
    size = scalar(step)

    def update(x):
        for k in range(3):
            residual[k, x] = v_m[k, x] - size * mapped_old[k, x]

    loop(0, span + 2 * level, update)

    def keep(x, fields):
        at = x - (level - 1)

        @pl.when((at >= 0) & (at < span))
        def _():
            for k in range(3):
                z_own[k, at] = own_of(fields[k])

    iterate(
        (span, depth), level, (MID, MID, MID), coup, store,
        lambda k, x: residual[k, x], lambda k, x: h_m[k, x], lambda x: root_m[x],
        (lambda at: lambda slot: kh_m[slot, at],), moved, moved_next, keep,
    )

    def image(x):
        out, _ = stencil(moved_next, x + 1, coup, lambda slot: kh_m[slot, x + 2])
        for k in range(3):
            mapped[k, x] = out[k]

    loop(0, span + 2 * level - 4, image)
    inner = level - 2
    parts = means_of(
        (span, depth), coup,
        lambda x: own_of(root_m[x + 4]),
        lambda k, x: h_m[k, x + 3], lambda k, x: mapped[k, x + inner - 1],
        lambda slot, x: kh_w[slot, x + REACH, own_rows(WIDE)], moved_own,
    )

    def dots(x, carry):
        gamma, delta, cross = carry
        for k in range(3):
            z = z_own[k, x]
            gamma = gamma + own_of(residual[k, x + level]) * z
            delta = delta + own_of(mapped[k, x + inner]) * z
            cross = cross + own_of(mapped_old[k, x + 4]) * z
        return gamma, delta, cross

    zero = jnp.zeros((8, depth), f32)
    dotted = lax.fori_loop(0, span, dots, (zero, zero, zero))
    scale = 1.0 / (span * 8 * depth)
    sums[...] = jnp.zeros_like(sums)
    for k in range(3):
        sums[k : k + 1] = row_sum(parts[k]) * scale
        sums[k + 3 : k + 4] = row_sum(dotted[k])
    msg[...] = send_row(to_lanes(sums[...]), devices)


def third_kernel(
    dims, counts, where, coup, beta, got, got_old, first, means, kh_m, h_m, root_m, kh_w, v_w, root_w,
    z_old, mapped_old, z_new, mapped_new, residual_old, lanczos, previous, locked,
    base, z_out, dir_out, scal, msg,
    moved, moved_next, residual, mapped, store, sums, locked_sums,
):
    span, depth, devices = dims
    level = REACH - 4
    total_old = row_sum(got_old[...])
    total = row_sum(got[...])
    gamma_old = pick(total_old, 3)
    delta_old = pick(total_old, 4)
    step_old = gamma_old / delta_old
    gamma = pick(total, 3)
    ratio = gamma / gamma_old
    delta = pick(total, 4) + 2.0 * ratio * pick(total, 5) + ratio * ratio * delta_old
    step = gamma / delta
    fresh = means[...] - step * (got[...] + ratio * got_old[...])
    padded = (first.shape[1] - LANES) // 3
    coarse_values(
        fresh,
        lambda k: first[:, LANES + k * padded : LANES + (k + 1) * padded],
        where, counts, store,
    )
    lane = lax.broadcasted_iota(jnp.int32, (1, LANES), 1)
    scal[...] = jnp.where(lane == 0, gamma, jnp.where(lane == 1, delta, 0.0))
    size, size_old, blend = scalar(step), scalar(step_old), scalar(ratio)

    def update(x):
        for k in range(3):
            mapped[k, x] = mapped_new[k, x] + blend * mapped_old[k, x + 2]
            residual[k, x] = residual_old[k, x + 2] - size * mapped[k, x]

    loop(0, span + 2 * level, update)

    def keep(x, fields):
        at = x - (level - 1)

        @pl.when((at >= 0) & (at < span))
        def _():
            for k in range(3):
                z_out[k, at] = own_of(fields[k])

    iterate(
        (span, depth), level, (MID, MID, OWN), coup, store,
        lambda k, x: residual[k, x], lambda k, x: h_m[k, x + 2], lambda x: root_m[x + 2],
        (lambda at: lambda slot: kh_m[slot, at + 2],), moved, moved_next, keep,
    )

    def finish(x, carry):
        gamma, delta, cross, with_base, with_z, with_dir, weight = carry
        own = own_rows(WIDE)
        image, _ = stencil(moved_next, x + 1, coup, lambda slot: kh_w[slot, x + REACH, own])
        inverse = 1.0 / root_w[x + REACH, own]
        for k in range(3):
            z = z_out[k, x]
            direction = z_new[k, x] + blend * z_old[k, x]
            partial = size_old * z_old[k, x] + size * direction
            vector = v_w[k, x + REACH, own]
            gamma = gamma + own_of(residual[k, x + level]) * z
            delta = delta + image[k] * z
            cross = cross + own_of(mapped[k, x + level]) * z
            with_base = with_base + vector * partial
            with_z = with_z + vector * z
            with_dir = with_dir + vector * direction
            weight = weight + lanczos[k, x] * lanczos[k, x]
            z_out[k, x] = z * inverse
            dir_out[k, x] = direction * inverse
            base[k, x] = partial * inverse - beta[0] * previous[k, x]
        return gamma, delta, cross, with_base, with_z, with_dir, weight

    zero = jnp.zeros((8, depth), f32)
    dotted = lax.fori_loop(0, span, finish, (zero,) * 7)
    sums[...] = jnp.zeros_like(sums)
    for k in range(7):
        sums[k : k + 1] = row_sum(dotted[k])

    def project(n):
        def body(x, carry):
            out = list(carry)
            for k in range(3):
                vector = locked[n, k, x]
                out[0] = out[0] + vector * base[k, x]
                out[1] = out[1] + vector * z_out[k, x]
                out[2] = out[2] + vector * dir_out[k, x]
                out[3] = out[3] + vector * lanczos[k, x]
            return tuple(out)

        four = lax.fori_loop(0, span, body, (zero,) * 4, unroll=True)
        rows = [row_sum(one) for one in four]
        locked_sums[n] = jnp.concatenate(rows, axis=0)

    count = locked.shape[0]
    loop(0, count, project)
    msg[:, :LANES] = send_row(to_lanes(sums[...]), devices)
    flat = locked_sums[...].reshape(count * 4, depth)
    msg[:, LANES:] = send_row(to_lanes(flat), devices)


def last_kernel(
    dims, got, scal, base, z, direction, lanczos, locked,
    remainder, out, msg,
    weights, sums,
):
    span, depth, devices = dims
    count = locked.shape[0]
    total = row_sum(got[...])
    head, tail = total[:, :LANES], total[:, LANES:]
    gamma_old, delta_old = pick(scal[...], 0), pick(scal[...], 1)
    gamma = pick(head, 0)
    ratio = gamma / gamma_old
    delta = pick(head, 1) + 2.0 * ratio * pick(head, 2) + ratio * ratio * delta_old
    step = gamma / delta
    inner = pick(head, 3) + step * (pick(head, 4) + ratio * pick(head, 5))
    alpha = inner / pick(head, 6)
    lane = lax.broadcasted_iota(jnp.int32, (1, LANES), 1)
    kind = lane % 4
    factor = jnp.where(kind == 0, 1.0, jnp.where(kind == 1, step, jnp.where(kind == 2, step * ratio, -alpha)))
    terms = jnp.where(lane < 4 * count, tail * factor, 0.0)
    row = jnp.where(lane == count, alpha, 0.0)
    for n in range(count):
        value = jnp.sum(jnp.where(lane // 4 == n, terms, 0.0), axis=1, keepdims=True)
        row = jnp.where(lane == n, value, row)
        weights[n] = scalar(value)
    out[...] = row
    size, both, shrink = scalar(step), scalar(step * ratio), scalar(alpha)

    def body(x, square):
        for k in range(3):
            rest = base[k, x] + size * z[k, x] + both * direction[k, x] - shrink * lanczos[k, x]
            taken = weights[0] * locked[0, k, x]
            for n in range(1, count):
                taken = taken + weights[n] * locked[n, k, x]
            rest = rest - taken
            remainder[k, x] = rest
            square = square + rest * rest
        return square

    square = lax.fori_loop(0, span, body, jnp.zeros((8, depth), f32))
    sums[...] = jnp.zeros_like(sums)
    sums[0:1] = row_sum(square)
    msg[...] = send_row(to_lanes(sums[...]), devices)


VMEM = pl.BlockSpec(memory_space=pltpu.VMEM)
SMEM = pl.BlockSpec(memory_space=pltpu.SMEM)


def call(kernel, name, outs, scratch, smem, *operands, limit=60 << 20):
    return pl.pallas_call(
        kernel,
        name=name,
        out_shape=[jax.ShapeDtypeStruct(shape, f32) for shape in outs],
        in_specs=[SMEM] * smem + [VMEM] * (len(operands) - smem),
        out_specs=[VMEM] * len(outs),
        scratch_shapes=scratch,
        compiler_params=pltpu.CompilerParams(vmem_limit_bytes=limit),
    )(*operands)


def swap_permutes(axis):
    count = lax.axis_size(axis)
    near = [(i, i ^ 1) for i in range(count) if i ^ 1 < count]
    far = [(i, ((i + 1) ^ 1) - 1) for i in range(count)]
    return near, [(i, j) for i, j in far if 0 <= j < count]


def exchange_rows(rows):
    return lax.all_to_all(rows, AXES, 0, 0, tiled=True)


def shards(
    lanczos_vector, previous_vector, previous_beta, locked_vectors, occupancy, young, couplings, coarse_inverse
):
    _, span, span_y, depth = lanczos_vector.shape
    counts = (lax.axis_size("slab"), lax.axis_size("block"))
    devices = counts[0] * counts[1]
    locked = locked_vectors.shape[0]
    halo = REACH + 1
    assert span_y == 8 and span >= halo and locked * 4 <= LANES
    slab, block = lax.axis_index("slab"), lax.axis_index("block")
    where = jnp.stack([slab, block]).astype(jnp.int32)
    coup = couplings.reshape(-1)

    density = jnp.where(occupancy == 1, 1.0, VOID_DENSITY).astype(f32)
    density = jnp.repeat(jnp.repeat(jnp.repeat(density, BRICK, 0), BRICK, 1), BRICK, 2)
    stiffness = density * young
    fields = jnp.concatenate([lanczos_vector, stiffness[None]], axis=0)

    odd = slab % 2
    near, far = swap_permutes("slab")
    upper = lax.slice_in_dim(fields, span - halo, span, axis=1)
    lower = lax.slice_in_dim(fields, 0, halo, axis=1)
    from_near = lax.ppermute(jnp.where(odd == 0, upper, lower), "slab", near)
    from_far = lax.ppermute(jnp.where(odd == 0, lower, upper), "slab", far)
    below = jnp.where(odd == 0, from_far, from_near)
    above = jnp.where(odd == 0, from_near, from_far)
    tall = jnp.concatenate([below, fields, above], axis=1)
    near, far = swap_permutes("block")
    side_near = lax.ppermute(tall, "block", near)
    side_far = lax.ppermute(tall, "block", far)

    dims = (span, depth, devices)
    wide = (span + 2 * REACH, WIDE[1], depth)
    mid = (span + 8, MID[1], depth)
    padded = -(-coarse_inverse.shape[1] // LANES) * LANES

    def scratch(*shape):
        return pltpu.VMEM(shape, f32)

    kh_w, h_w, v_w, root_w, kh_m, h_m, v_m, root_m, msg = call(
        functools.partial(setup_kernel, dims),
        "setup",
        [(6, *wide), (3, *wide), (3, *wide), wide, (6, *mid), (3, *mid), (3, *mid), mid, (devices, LANES + 3 * padded)],
        [
            scratch(9, span + 2 * halo, WIDE[1], depth),
            scratch(span + 2 * halo, WIDE[1], depth),
            scratch(27, span + 2, 8, depth),
            scratch(8, depth),
        ],
        2,
        where, coup, side_near, side_far, tall, coarse_inverse,
    )
    first = exchange_rows(msg)

    own = (3, span, 8, depth)
    store = pltpu.SMEM((27,), f32)
    z_0, mapped_0, msg = call(
        functools.partial(first_kernel, dims, counts),
        "first",
        [own, (3, *mid), (devices, LANES)],
        [
            scratch(27, *wide),
            scratch(27, span + 2 * REACH - 2, MID[1], depth),
            scratch(27, span + 2, 8, depth),
            store,
            scratch(8, depth),
        ],
        2,
        where, coup, first, kh_w, h_w, v_w, root_w, kh_m, h_m,
    )
    got_0 = exchange_rows(msg)

    level = REACH - 2
    inner = (3, span + 2 * level - 4, MID[1], depth)
    z_1, mapped_1, residual, means, msg = call(
        functools.partial(second_kernel, dims, counts),
        "second",
        [own, inner, (3, *mid), (devices, LANES), (devices, LANES)],
        [
            scratch(27, *mid),
            scratch(27, span + 2 * level - 2, MID[1], depth),
            scratch(27, span + 2, 8, depth),
            store,
            scratch(8, depth),
        ],
        2,
        where, coup, got_0, first, kh_m, h_m, v_m, root_m, kh_w, z_0, mapped_0,
    )
    got_1 = exchange_rows(msg)

    level = REACH - 4
    base, z_2, direction, scal, msg = call(
        functools.partial(third_kernel, dims, counts),
        "third",
        [own, own, own, (1, LANES), (devices, 2 * LANES)],
        [
            scratch(27, span + 2 * level, MID[1], depth),
            scratch(27, span + 2 * level - 2, 8, depth),
            scratch(3, span + 2 * level, MID[1], depth),
            scratch(3, span + 2 * level, MID[1], depth),
            store,
            scratch(8, depth),
            scratch(locked, 4, depth),
        ],
        3,
        where, coup, previous_beta.reshape(1), got_1, got_0, first, means, kh_m, h_m, root_m, kh_w, v_w, root_w,
        z_0, mapped_0, z_1, mapped_1, residual, lanczos_vector, previous_vector, locked_vectors,
    )
    got_2 = exchange_rows(msg)

    remainder, row, msg = call(
        functools.partial(last_kernel, dims),
        "last",
        [own, (1, LANES), (devices, LANES)],
        [pltpu.SMEM((locked,), f32), scratch(8, depth)],
        0,
        got_2, scal, base, z_2, direction, lanczos_vector, locked_vectors,
    )
    square = jnp.sum(exchange_rows(msg)[:, 0])
    cell_count = 3.0 * span * span_y * depth * devices
    beta_norm = jnp.sqrt(square / cell_count)
    return remainder, jnp.stack([row[0, locked], beta_norm]), row[0, :locked]


def solution(mesh):
    in_specs = (
        P(None, "slab", "block", None),
        P(None, "slab", "block", None),
        P(),
        P(None, None, "slab", "block", None),
        P("slab", "block", None),
        P("slab", "block", None),
        P(),
        P(("slab", "block"), None),
    )
    out_specs = (P(None, "slab", "block", None), P(), P())
    return jax.shard_map(shards, mesh=mesh, in_specs=in_specs, out_specs=out_specs, check_vma=False)
```

```python
import functools

import jax
import jax.numpy as jnp
from jax import lax
from jax.experimental import pallas as pl
from jax.experimental.pallas import tpu as pltpu
from jax.sharding import PartitionSpec as P

BRICK = 8
ITERS = 3
SHIFT_MASS = 0.02
SMOOTH_WEIGHT = 0.5
VOID_DENSITY = 0.1

AXES = ("slab", "block")
LANES = 128
WIDE = (8, 24)
MID = (4, 16)
OWN = (0, 8)
REACH = 2 * ITERS
PAIRS = [(n // 9 - 1, n // 3 % 3 - 1, n % 3 - 1) for n in range(13)]
f32 = jnp.float32


def along_z(field, dz):
    rows, depth = field.shape
    lane = lax.broadcasted_iota(jnp.int32, (rows, LANES), 1)
    chunks = [field[:, low : low + LANES] for low in range(0, depth, LANES)]
    turned = [pltpu.roll(chunk, (-dz) % LANES, 1) for chunk in chunks]
    edge = 0 if dz < 0 else LANES - 1
    out = []
    for number, chunk in enumerate(turned):
        other = number + dz
        filler = turned[other] if 0 <= other < len(turned) else 0.0
        out.append(jnp.where(lane == edge, filler, chunk))
    return jnp.concatenate(out, axis=1)


def shift_store(dest, at, fields, source, target):
    src_off, src_rows = source
    dst_off, dst_rows = target
    for comp, field in enumerate(fields):
        for dy in (-1, 0, 1):
            shift = src_off - dst_off + dy
            moved = field if shift == 0 else pltpu.roll(field, (-shift) % src_rows, 0)
            if dst_rows != src_rows:
                moved = moved[:dst_rows]
            for dz in (-1, 0, 1):
                out = moved if dz == 0 else along_z(moved, dz)
                dest[((dy + 1) * 3 + dz + 1) * len(fields) + comp, at] = out


def pair_slots(pair):
    dx, dy, dz = pair
    return dx, (dy + 1) * 3 + dz + 1, (1 - dy) * 3 + 1 - dz


def stencil(moved, at, coup, center):
    near = [moved[4 * 3 + c, at] for c in range(3)]
    total = [center(i) * value for i, value in enumerate(six_of(near))]
    for number, pair in enumerate(PAIRS):
        dx, plus, minus = pair_slots(pair)
        sums = [moved[plus * 3 + c, at + dx] + moved[minus * 3 + c, at - dx] for c in range(3)]
        for i, value in enumerate(six_of(sums)):
            total[i] = total[i] + coup[number * 6 + i] * value
    out = [
        total[0] + (total[3] + total[4]),
        total[1] + (total[3] + total[5]),
        total[2] + (total[4] + total[5]),
    ]
    return out, near


def six_of(three):
    return [*three, three[0] + three[1], three[0] + three[2], three[1] + three[2]]


def loop(low, high, body):
    def step(i, carry):
        body(i)
        return carry

    lax.fori_loop(low, high, step, 0)


def row_sum(x):
    return jnp.sum(x, axis=0, keepdims=True)


def to_lanes(rows):
    column = jnp.sum(rows, axis=1, keepdims=True)
    count = rows.shape[0]
    here = lax.broadcasted_iota(jnp.int32, (count, LANES), 0)
    lane = lax.broadcasted_iota(jnp.int32, (count, LANES), 1)
    return row_sum(jnp.where(here == lane, column, 0.0))


def pick(row, index):
    lane = lax.broadcasted_iota(jnp.int32, row.shape, 1)
    return jnp.sum(jnp.where(lane == index, row, 0.0), axis=1, keepdims=True)


def scalar(one):
    return one[0, 0]


def coarse_values(means, rows_of, where, counts, store):
    total = None
    for k in range(3):
        part = row_sum(rows_of(k) * means[:, k : k + 1])
        total = part if total is None else total + part
    for bx in range(3):
        for by in range(3):
            spot = (where[0] + bx - 1) * counts[1] + where[1] + by - 1
            for k in range(3):
                store[(bx * 3 + by) * 3 + k] = scalar(pick(total, spot * 3 + k))


def correction(store, x, k, layout, span, depth):
    off, rows = layout
    base = lax.div(x + span, span) * 9 + k
    row = lax.broadcasted_iota(jnp.int32, (rows, depth), 0)
    high = jnp.where(row < off + 8, store[base + 3], store[base + 6])
    return jnp.where(row < off, store[base], high)


def send(msg, low, row, count):
    width = row.shape[1]
    msg[:, :, low : low + width] = jnp.broadcast_to(row.reshape(1, 1, width), (count, 1, width))


def side_rows(where, even, odd, mid):
    flip = where[1] % 2 == 1

    def wide(comp, x):
        first, second = even[comp, x], odd[comp, x]
        low = jnp.where(flip, first, second)
        high = jnp.where(flip, second, first)
        return jnp.concatenate([low, mid[comp, x], high], axis=0)

    return wide


def repack(field):
    return pltpu.roll(field, WIDE[1] - (WIDE[0] - MID[0]), 0)[: MID[1]]


def own_of(field):
    return pltpu.roll(field, MID[1] - MID[0], 0)[:8]


def center_row(moved_root, at, root, coup):
    total = [None] * 6
    for number, pair in enumerate(PAIRS):
        dx, plus, minus = pair_slots(pair)
        both = moved_root[plus, at + dx] + moved_root[minus, at - dx]
        for i in range(6):
            term = coup[number * 6 + i] * both
            total[i] = term if total[i] is None else total[i] + term
    inside = root > 0.0
    inverse = jnp.where(inside, 1.0 / jnp.where(inside, root, 1.0), 0.0)
    center = [-total[i] * inverse for i in range(6)]
    center[:3] = [one + SHIFT_MASS for one in center[:3]]
    whole = [
        center[0] + (center[3] + center[4]),
        center[1] + (center[3] + center[5]),
        center[2] + (center[4] + center[5]),
    ]
    half = [jnp.where(inside, SMOOTH_WEIGHT / one, 0.0) for one in whole]
    return center, half, inverse


def setup_kernel(
    dims, where, coup, even, odd, mid, cinv,
    kh_w, h_w, v_w, root_w, kh_m, h_m, v_m, root_m, kh_o, v_o, root_o, msg,
    moved_root, root_all, moved_own, sums,
):
    span, depth, devices = dims
    halo = REACH + 1
    wide = side_rows(where, even, odd, mid)

    def roots(x):
        root = jnp.sqrt(wide(3, x))
        root_all[x] = root
        shift_store(moved_root, x, [root], WIDE, WIDE)

    def diagonals(x, also_mid, also_own):
        at = x + 1
        root = root_all[at]
        center, half, inverse = center_row(moved_root, at, root, coup)
        m, o = x - (REACH - 4), x - REACH
        vectors = [wide(k, at) * inverse for k in range(3)]
        root_w[x] = root
        for k in range(3):
            h_w[k, x] = half[k]
            v_w[k, x] = vectors[k]
        for i in range(6):
            kh_w[i, x] = center[i]
        if also_mid:
            root_m[m] = repack(root)
            for k in range(3):
                h_m[k, m] = repack(half[k])
                v_m[k, m] = repack(vectors[k])
            for i in range(6):
                kh_m[i, m] = repack(center[i])
        if also_own:
            own = slice(WIDE[0], WIDE[0] + 8)
            root_o[o] = root[own]
            for k in range(3):
                v_o[k, o] = vectors[k][own]
            for i in range(6):
                kh_o[i, o] = center[i][own]

    loop(0, span + 2 * halo, roots)

    def both(also_mid, also_own):
        def body(x):
            diagonals(x, also_mid, also_own)

        return body

    edge = REACH - 4
    loop(0, edge, both(False, False))
    loop(edge, REACH, both(True, False))
    loop(REACH, REACH + span, both(True, True))
    loop(REACH + span, edge + span + 8, both(True, False))
    loop(edge + span + 8, span + 2 * REACH, both(False, False))

    def smooth(x):
        at = x + REACH - 1
        shift_store(moved_own, x, [h_w[k, at] * v_w[k, at] for k in range(3)], WIDE, OWN)

    loop(0, span + 2, smooth)

    def remain(x, carry):
        for i in (2 * x, 2 * x + 1):
            image, _ = stencil(moved_own, i + 1, coup, lambda slot: kh_o[slot, i])
            carry = tuple(carry[k] + root_o[i] * (v_o[k, i] - image[k]) for k in range(3))
        return carry

    zero = jnp.zeros((8, depth), f32)
    parts = lax.fori_loop(0, span // 2, remain, (zero, zero, zero))
    sums[...] = jnp.zeros_like(sums)
    for k in range(3):
        sums[k : k + 1] = row_sum(parts[k])
    send(msg, 0, to_lanes(sums[...]) * (1.0 / (span * 8 * depth)), devices)
    width = cinv.shape[1]
    padded = (msg.shape[2] - LANES) // 3
    for k in range(3):
        row = cinv[k : k + 1]
        if padded != width:
            row = jnp.concatenate([row, jnp.zeros((1, padded - width), f32)], axis=1)
        send(msg, LANES + k * padded, row, devices)


def iterate(dims, level, layouts, coup, store, residual, half, root, center, moved, moved_next, z_all, image):
    span, depth = dims
    source, first, second = layouts

    def begin(x):
        fields = []
        for k in range(3):
            fix = correction(store, x - level, k, source, span, depth)
            fields.append(half(k, x) * residual(k, x) + root(x) * fix)
        shift_store(moved, x, fields, source, first)

    def middle(x):
        at = x + 1
        out, near = stencil(moved, at, coup, center(at))
        fields = [near[k] + half(k, at) * (residual(k, at) - out[k]) for k in range(3)]
        for k in range(3):
            z_all[k, x] = fields[k]
        shift_store(moved_next, x, fields, first, second)

    def both(x):
        begin(x + 2)
        middle(x)

    loop(0, span + 2 * level, begin)
    loop(0, span + 2 * level - 2, middle)
    if image is not None:
        loop(0, span + 2 * level - 4, image)


def own_rows(layout):
    return slice(layout[0], layout[0] + 8)


def means_of(dims, coup, root, half, mapped, center, moved_own):
    span, depth = dims

    def begin(x):
        shift_store(moved_own, x, [half(k, x) * mapped(k, x) for k in range(3)], MID, OWN)

    def body(x, carry):
        for i in (2 * x, 2 * x + 1):
            image, _ = stencil(moved_own, i + 1, coup, lambda slot: center(slot, i))
            carry = tuple(carry[k] + root(i) * (own_of(mapped(k, i + 1)) - image[k]) for k in range(3))
        return carry

    loop(0, span + 2, begin)
    zero = jnp.zeros((8, depth), f32)
    return lax.fori_loop(0, span // 2, body, (zero, zero, zero))


def first_kernel(
    dims, counts, where, coup, got, kh_w, h_w, v_w, root_w, kh_m, h_m, kh_o, v_o, root_o,
    z_own, mapped, msg,
    moved, moved_next, moved_own, z_all, store, sums,
):
    span, depth, devices = dims
    level = REACH
    padded = (got.shape[2] - LANES) // 3
    coarse_values(
        got[:, 0, :LANES],
        lambda k: got[:, 0, LANES + k * padded : LANES + (k + 1) * padded],
        where, counts, store,
    )

    def image(x):
        out, _ = stencil(moved_next, x + 1, coup, lambda i: kh_m[i, x])
        for k in range(3):
            mapped[k, x] = out[k]

    iterate(
        (span, depth), level, (WIDE, WIDE, MID), coup, store,
        lambda k, x: v_w[k, x], lambda k, x: h_w[k, x], lambda x: root_w[x],
        (lambda at: lambda i: kh_w[i, at]), moved, moved_next, z_all, image,
    )
    inner = level - 2
    parts = means_of(
        (span, depth), coup, lambda x: root_o[x],
        lambda k, x: h_m[k, x + 3], lambda k, x: mapped[k, x + inner - 1],
        lambda i, x: kh_o[i, x], moved_own,
    )

    def dots(x, carry):
        gamma, delta = carry
        for k in range(3):
            z = z_all[k, x + level - 1, own_rows(WIDE)]
            z_own[k, x] = z
            gamma = gamma + v_o[k, x] * z
            delta = delta + own_of(mapped[k, x + inner]) * z
        return gamma, delta

    zero = jnp.zeros((8, depth), f32)
    gamma, delta = lax.fori_loop(0, span, dots, (zero, zero))
    scale = 1.0 / (span * 8 * depth)
    sums[...] = jnp.zeros_like(sums)
    for k in range(3):
        sums[k : k + 1] = row_sum(parts[k]) * scale
    sums[3:4] = row_sum(gamma)
    sums[4:5] = row_sum(delta)
    send(msg, 0, to_lanes(sums[...]), devices)


def second_kernel(
    dims, counts, where, coup, got, first, kh_m, h_m, v_m, root_m, kh_o, root_o, mapped_old,
    z_own, mapped, residual, means, msg,
    moved, moved_next, moved_own, z_all, store, sums,
):
    span, depth, devices = dims
    level = REACH - 2
    total = row_sum(got[:, 0])
    gamma = pick(total, 3)
    step = gamma / pick(total, 4)
    padded = (first.shape[2] - LANES) // 3
    fresh = first[:, 0, :LANES] - step * got[:, 0]
    means[...] = fresh
    coarse_values(
        fresh,
        lambda k: first[:, 0, LANES + k * padded : LANES + (k + 1) * padded],
        where, counts, store,
    )
    size = scalar(step)

    def rest(k, x):
        return v_m[k, x] - size * mapped_old[k, x]

    def image(x):
        out, _ = stencil(moved_next, x + 1, coup, lambda i: kh_m[i, x + 2])
        for k in range(3):
            mapped[k, x] = out[k]

    iterate(
        (span, depth), level, (MID, MID, MID), coup, store,
        rest, lambda k, x: h_m[k, x], lambda x: root_m[x],
        (lambda at: lambda i: kh_m[i, at]), moved, moved_next, z_all, image,
    )
    inner = level - 2
    parts = means_of(
        (span, depth), coup, lambda x: root_o[x],
        lambda k, x: h_m[k, x + 3], lambda k, x: mapped[k, x + inner - 1],
        lambda i, x: kh_o[i, x], moved_own,
    )

    def dots(x, carry):
        gamma, delta, cross = carry
        for k in range(3):
            z = own_of(z_all[k, x + level - 1])
            z_own[k, x] = z
            gamma = gamma + own_of(rest(k, x + level)) * z
            delta = delta + own_of(mapped[k, x + inner]) * z
            cross = cross + own_of(mapped_old[k, x + 4]) * z
        return gamma, delta, cross

    zero = jnp.zeros((8, depth), f32)
    dotted = lax.fori_loop(0, span, dots, (zero, zero, zero))

    def keep(x):
        for k in range(3):
            residual[k, x] = rest(k, x + inner)

    loop(0, span + 2 * inner, keep)
    scale = 1.0 / (span * 8 * depth)
    sums[...] = jnp.zeros_like(sums)
    for k in range(3):
        sums[k : k + 1] = row_sum(parts[k]) * scale
        sums[k + 3 : k + 4] = row_sum(dotted[k])
    send(msg, 0, to_lanes(sums[...]), devices)


def third_kernel(
    dims, counts, where, coup, got, got_old, first, means, kh_m, h_m, root_m, kh_o, v_o, root_o,
    z_old, mapped_old, z_new, mapped_new, residual_old, lanczos, previous, locked,
    base, z_out, dir_out, scal, msg,
    moved, moved_next, residual, mapped, z_all, store, sums, locked_sums,
):
    span, depth, devices = dims
    level = REACH - 4
    total_old = row_sum(got_old[:, 0])
    total = row_sum(got[:, 0])
    gamma_old = pick(total_old, 3)
    delta_old = pick(total_old, 4)
    step_old = gamma_old / delta_old
    gamma = pick(total, 3)
    ratio = gamma / gamma_old
    delta = pick(total, 4) + 2.0 * ratio * pick(total, 5) + ratio * ratio * delta_old
    step = gamma / delta
    fresh = means[...] - step * (got[:, 0] + ratio * got_old[:, 0])
    padded = (first.shape[2] - LANES) // 3
    coarse_values(
        fresh,
        lambda k: first[:, 0, LANES + k * padded : LANES + (k + 1) * padded],
        where, counts, store,
    )
    lane = lax.broadcasted_iota(jnp.int32, (1, LANES), 1)
    scal[...] = jnp.where(lane == 0, gamma, jnp.where(lane == 1, delta, 0.0))
    size, size_old, blend = scalar(step), scalar(step_old), scalar(ratio)

    def update(x):
        for k in range(3):
            mapped[k, x] = mapped_new[k, x] + blend * mapped_old[k, x + 2]
            residual[k, x] = residual_old[k, x] - size * mapped[k, x]

    loop(0, span + 2 * level, update)
    iterate(
        (span, depth), level, (MID, MID, OWN), coup, store,
        lambda k, x: residual[k, x], lambda k, x: h_m[k, x + 2], lambda x: root_m[x + 2],
        (lambda at: lambda i: kh_m[i, at + 2]), moved, moved_next, z_all, None,
    )

    def finish(x, carry):
        gamma, delta, cross, with_base, with_z, with_dir, weight = carry
        image, near = stencil(moved_next, x + 1, coup, lambda i: kh_o[i, x])
        inverse = 1.0 / root_o[x]
        for k in range(3):
            z = near[k]
            direction = z_new[k, x] + blend * z_old[k, x]
            partial = size_old * z_old[k, x] + size * direction
            vector = v_o[k, x]
            gamma = gamma + own_of(residual[k, x + level]) * z
            delta = delta + image[k] * z
            cross = cross + own_of(mapped[k, x + level]) * z
            with_base = with_base + vector * partial
            with_z = with_z + vector * z
            with_dir = with_dir + vector * direction
            weight = weight + lanczos[k, x] * lanczos[k, x]
            z_out[k, x] = z * inverse
            dir_out[k, x] = direction * inverse
            base[k, x] = partial * inverse - coup[6 * len(PAIRS)] * previous[k, x]
        return gamma, delta, cross, with_base, with_z, with_dir, weight

    zero = jnp.zeros((8, depth), f32)
    dotted = lax.fori_loop(0, span, finish, (zero,) * 7)
    sums[...] = jnp.zeros_like(sums)
    for k in range(7):
        sums[k : k + 1] = row_sum(dotted[k])

    def project(n):
        def body(x, carry):
            out = list(carry)
            for k in range(3):
                vector = locked[n, k, x]
                out[0] = out[0] + vector * base[k, x]
                out[1] = out[1] + vector * z_out[k, x]
                out[2] = out[2] + vector * dir_out[k, x]
                out[3] = out[3] + vector * lanczos[k, x]
            return tuple(out)

        four = lax.fori_loop(0, span, body, (zero,) * 4, unroll=True)
        rows = [row_sum(one) for one in four]
        locked_sums[n] = jnp.concatenate(rows, axis=0)

    count = locked.shape[0]
    loop(0, count, project)
    send(msg, 0, to_lanes(sums[...]), devices)
    flat = locked_sums[...].reshape(count * 4, depth)
    send(msg, LANES, to_lanes(flat), devices)


def last_kernel(
    dims, got, scal, base, z, direction, lanczos, locked,
    remainder, weights, found, msg,
    sums,
):
    span, depth, devices = dims
    count = locked.shape[0]
    total = row_sum(got[:, 0])
    head, tail = total[:, :LANES], total[:, LANES:]
    gamma_old, delta_old = pick(scal[...], 0), pick(scal[...], 1)
    gamma = pick(head, 0)
    ratio = gamma / gamma_old
    delta = pick(head, 1) + 2.0 * ratio * pick(head, 2) + ratio * ratio * delta_old
    step = gamma / delta
    inner = pick(head, 3) + step * (pick(head, 4) + ratio * pick(head, 5))
    alpha = inner / pick(head, 6)
    lane = lax.broadcasted_iota(jnp.int32, (1, LANES), 1)
    kind = lane % 4
    factor = jnp.where(kind == 0, 1.0, jnp.where(kind == 1, step, jnp.where(kind == 2, step * ratio, -alpha)))
    terms = jnp.where(lane < 4 * count, tail * factor, 0.0)
    for n in range(count):
        value = jnp.sum(jnp.where(lane // 4 == n, terms, 0.0), axis=1, keepdims=True)
        weights[n] = scalar(value)
    found[0] = scalar(alpha)
    size, both, shrink = scalar(step), scalar(step * ratio), scalar(alpha)

    def body(x, square):
        for k in range(3):
            rest = base[k, x] + size * z[k, x] + both * direction[k, x] - shrink * lanczos[k, x]
            taken = weights[0] * locked[0, k, x]
            for n in range(1, count):
                taken = taken + weights[n] * locked[n, k, x]
            rest = rest - taken
            remainder[k, x] = rest
            square = square + rest * rest
        return square

    square = lax.fori_loop(0, span, body, jnp.zeros((8, depth), f32))
    sums[...] = jnp.zeros_like(sums)
    sums[0:1] = row_sum(square)
    send(msg, 0, to_lanes(sums[...]), devices)


def closing_kernel(cells, got, found, out):
    total = jnp.sum(row_sum(got[:, 0])[:, :8], axis=1, keepdims=True)
    out[0] = found[0]
    out[1] = scalar(jnp.sqrt(total / cells))


VMEM = pl.BlockSpec(memory_space=pltpu.VMEM)
SMEM = pl.BlockSpec(memory_space=pltpu.SMEM)


def call(kernel, name, outs, scratch, *operands, limit=60 << 20):
    return pl.pallas_call(
        kernel,
        name=name,
        out_shape=[jax.ShapeDtypeStruct(shape, f32) for shape in outs],
        in_specs=[SMEM if len(operand.shape) == 1 else VMEM for operand in operands],
        out_specs=[SMEM if len(shape) == 1 else VMEM for shape in outs],
        scratch_shapes=scratch,
        compiler_params=pltpu.CompilerParams(vmem_limit_bytes=limit),
    )(*operands)


def swap_permutes(axis):
    count = lax.axis_size(axis)
    near = [(i, i ^ 1) for i in range(count) if i ^ 1 < count]
    far = [(i, ((i + 1) ^ 1) - 1) for i in range(count)]
    return near, [(i, j) for i, j in far if 0 <= j < count]


def exchange_rows(rows):
    return lax.all_to_all(rows, AXES, 0, 0, tiled=True)


def shards(
    lanczos_vector, previous_vector, previous_beta, locked_vectors, occupancy, young, couplings, coarse_inverse
):
    _, span, span_y, depth = lanczos_vector.shape
    counts = (lax.axis_size("slab"), lax.axis_size("block"))
    devices = counts[0] * counts[1]
    locked = locked_vectors.shape[0]
    halo = REACH + 1
    assert span_y == 8 and span >= halo and locked * 4 <= LANES
    slab, block = lax.axis_index("slab"), lax.axis_index("block")
    where = jnp.stack([slab, block]).astype(jnp.int32)
    flat = -couplings.reshape(-1, 9)
    a, b, c = flat[:, 1], flat[:, 2], flat[:, 5]
    six = jnp.stack([flat[:, 0] - a - b, flat[:, 4] - a - c, flat[:, 8] - b - c, a, b, c], axis=1)
    coup = jnp.concatenate([six.reshape(-1), previous_beta.reshape(1)])

    density = jnp.where(occupancy == 1, 1.0, VOID_DENSITY).astype(f32)
    density = jnp.repeat(jnp.repeat(jnp.repeat(density, BRICK, 0), BRICK, 1), BRICK, 2)
    stiffness = density * young
    fields = jnp.concatenate([lanczos_vector, stiffness[None]], axis=0)

    odd = slab % 2
    near, far = swap_permutes("slab")
    upper = lax.slice_in_dim(fields, span - halo, span, axis=1)
    lower = lax.slice_in_dim(fields, 0, halo, axis=1)
    from_near = lax.ppermute(jnp.where(odd == 0, upper, lower), "slab", near)
    from_far = lax.ppermute(jnp.where(odd == 0, lower, upper), "slab", far)
    below = jnp.where(odd == 0, from_far, from_near)
    above = jnp.where(odd == 0, from_near, from_far)
    tall = jnp.concatenate([below, fields, above], axis=1)
    near, far = swap_permutes("block")
    tall, where, coup, coarse_inverse = lax.optimization_barrier((tall, where, coup, coarse_inverse))
    side_near = lax.ppermute(tall, "block", near)
    side_far = lax.ppermute(tall, "block", far)

    dims = (span, depth, devices)
    wide = (span + 2 * REACH, WIDE[1], depth)
    mid = (span + 8, MID[1], depth)
    own = (3, span, 8, depth)
    padded = -(-coarse_inverse.shape[1] // LANES) * LANES
    row = (devices, 1, LANES)

    def scratch(*shape):
        return pltpu.VMEM(shape, f32)

    kh_w, h_w, v_w, root_w, kh_m, h_m, v_m, root_m, kh_o, v_o, root_o, msg = call(
        functools.partial(setup_kernel, dims),
        "setup",
        [
            (6, *wide), (3, *wide), (3, *wide), wide, (6, *mid), (3, *mid), (3, *mid), mid,
            (6, *own[1:]), own, own[1:], (devices, 1, LANES + 3 * padded),
        ],
        [
            scratch(9, span + 2 * halo + 1, WIDE[1], depth),
            scratch(span + 2 * halo + 1, WIDE[1], depth),
            scratch(27, span + 2, 8, depth),
            scratch(8, depth),
        ],
        where, coup, side_near, side_far, tall, coarse_inverse, limit=9 << 20,
    )
    first = exchange_rows(msg)

    store = pltpu.SMEM((27,), f32)
    z_0, mapped_0, msg = call(
        functools.partial(first_kernel, dims, counts),
        "first",
        [own, (3, *mid), row],
        [
            scratch(27, *wide),
            scratch(27, span + 2 * REACH - 2, MID[1], depth),
            scratch(27, span + 2, 8, depth),
            scratch(3, span + 2 * REACH - 2, WIDE[1], depth),
            store,
            scratch(8, depth),
        ],
        where, coup, first, kh_w, h_w, v_w, root_w, kh_m, h_m, kh_o, v_o, root_o, limit=28 << 20,
    )
    got_0 = exchange_rows(msg)

    level = REACH - 2
    inner = (3, span + 2 * level - 4, MID[1], depth)
    z_1, mapped_1, residual, means, msg = call(
        functools.partial(second_kernel, dims, counts),
        "second",
        [own, inner, inner, (devices, LANES), row],
        [
            scratch(27, *mid),
            scratch(27, span + 2 * level - 2, MID[1], depth),
            scratch(27, span + 2, 8, depth),
            scratch(3, span + 2 * level - 2, MID[1], depth),
            store,
            scratch(8, depth),
        ],
        where, coup, got_0, first, kh_m, h_m, v_m, root_m, kh_o, root_o, mapped_0, limit=18 << 20,
    )
    got_1 = exchange_rows(msg)

    level = REACH - 4
    base, z_2, direction, scal, msg = call(
        functools.partial(third_kernel, dims, counts),
        "third",
        [own, own, own, (1, LANES), (devices, 1, 2 * LANES)],
        [
            scratch(27, span + 2 * level, MID[1], depth),
            scratch(27, span + 2 * level - 2, 8, depth),
            scratch(3, span + 2 * level, MID[1], depth),
            scratch(3, span + 2 * level, MID[1], depth),
            scratch(3, span + 2 * level - 2, MID[1], depth),
            store,
            scratch(8, depth),
            scratch(locked, 4, depth),
        ],
        where, coup, got_1, got_0, first, means, kh_m, h_m, root_m, kh_o, v_o, root_o,
        z_0, mapped_0, z_1, mapped_1, residual, lanczos_vector, previous_vector, locked_vectors, limit=16 << 20,
    )
    got_2 = exchange_rows(msg)

    remainder, projections, found, msg = call(
        functools.partial(last_kernel, dims),
        "last",
        [own, (locked,), (1,), row],
        [scratch(8, depth)],
        got_2, scal, base, z_2, direction, lanczos_vector, locked_vectors, limit=6 << 20,
    )
    (coefficients,) = call(
        functools.partial(closing_kernel, 3.0 * span * span_y * depth * devices),
        "closing",
        [(2,)],
        [],
        exchange_rows(msg), found, limit=4 << 20,
    )
    return remainder, coefficients, projections


def solution(mesh):
    in_specs = (
        P(None, "slab", "block", None),
        P(None, "slab", "block", None),
        P(),
        P(None, None, "slab", "block", None),
        P("slab", "block", None),
        P("slab", "block", None),
        P(),
        P(("slab", "block"), None),
    )
    out_specs = (P(None, "slab", "block", None), P(), P())
    return jax.shard_map(shards, mesh=mesh, in_specs=in_specs, out_specs=out_specs, check_vma=False)
```

```python
import functools

import jax
import jax.numpy as jnp
from jax import lax
from jax.experimental import pallas as pl
from jax.experimental.pallas import tpu as pltpu
from jax.sharding import PartitionSpec as P

BRICK = 8
ITERS = 3
SHIFT_MASS = 0.02
SMOOTH_WEIGHT = 0.5
VOID_DENSITY = 0.1

AXES = ("slab", "block")
LANES = 128
WIDE = (8, 24)
MID = (4, 16)
OWN = (0, 8)
REACH = 2 * ITERS
HALF = [(-1, -1), (-1, 0), (-1, 1), (0, -1)]
f32 = jnp.float32


def along_z(chunks, dz):
    lane = lax.broadcasted_iota(jnp.int32, chunks[0].shape, 1)
    turned = [pltpu.roll(chunk, (-dz) % LANES, 1) for chunk in chunks]
    edge = 0 if dz < 0 else LANES - 1
    out = []
    for number, chunk in enumerate(turned):
        other = number + dz
        filler = turned[other] if 0 <= other < len(turned) else 0.0
        out.append(jnp.where(lane == edge, filler, chunk))
    return out


def shift_store(dest, at, fields, source, target):
    src_off, src_rows = source
    dst_off, dst_rows = target
    for comp, field in enumerate(fields):
        for dy in (-1, 0, 1):
            shift = src_off - dst_off + dy
            moved = field if shift == 0 else pltpu.roll(field, (-shift) % src_rows, 0)
            if dst_rows != src_rows:
                moved = moved[:dst_rows]
            dest[(dy + 1) * len(fields) + comp, at] = moved


def gather_z(parts):
    flat, up, down = zip(*parts)
    above, below = along_z(up, 1), along_z(down, -1)
    return jnp.concatenate([a + (b + c) for a, b, c in zip(flat, above, below)], axis=1)


def stencil(moved, at, coup, center):
    depth = moved.shape[3]
    parts = [[], [], []]
    rows = []
    for low in range(0, depth, LANES):
        cut = slice(low, low + LANES)
        near = [moved[3 + c, at, :, cut] for c in range(3)]
        rows.append(near)
        flat, up, down = [], [], [None] * 6
        for i, value in enumerate(six_of(near)):
            flat.append(center(i, cut) * value)
            up.append(coup[18 * len(HALF) + i] * value)
        for q, (dx, dy) in enumerate(HALF):
            plus = [moved[(dy + 1) * 3 + c, at + dx, :, cut] for c in range(3)]
            minus = [moved[(1 - dy) * 3 + c, at - dx, :, cut] for c in range(3)]
            for i, value in enumerate(six_of([p + m for p, m in zip(plus, minus)])):
                flat[i] = flat[i] + coup[q * 18 + i] * value
                up[i] = up[i] + coup[q * 18 + 6 + i] * value
            for i, value in enumerate(six_of([p - m for p, m in zip(plus, minus)])):
                term = coup[q * 18 + 12 + i] * value
                down[i] = term if down[i] is None else down[i] + term
        flat, up, down = fold(flat), fold(up), fold(down)
        for k in range(3):
            parts[k].append((flat[k], up[k] + down[k], up[k] - down[k]))
    near = [jnp.concatenate([row[k] for row in rows], axis=1) for k in range(3)]
    return [gather_z(one) for one in parts], near


def fold(six):
    return [six[0] + (six[3] + six[4]), six[1] + (six[3] + six[5]), six[2] + (six[4] + six[5])]


def six_of(three):
    return [*three, three[0] + three[1], three[0] + three[2], three[1] + three[2]]


def loop(low, high, body):
    def step(i, carry):
        body(i)
        return carry

    lax.fori_loop(low, high, step, 0)


def row_sum(x):
    return jnp.sum(x, axis=0, keepdims=True)


def to_lanes(rows):
    column = jnp.sum(rows, axis=1, keepdims=True)
    count = rows.shape[0]
    here = lax.broadcasted_iota(jnp.int32, (count, LANES), 0)
    lane = lax.broadcasted_iota(jnp.int32, (count, LANES), 1)
    return row_sum(jnp.where(here == lane, column, 0.0))


def pick(row, index):
    lane = lax.broadcasted_iota(jnp.int32, row.shape, 1)
    return jnp.sum(jnp.where(lane == index, row, 0.0), axis=1, keepdims=True)


def scalar(one):
    return one[0, 0]


def coarse_values(means, rows_of, where, counts, store):
    total = None
    for k in range(3):
        part = row_sum(rows_of(k) * means[:, k : k + 1])
        total = part if total is None else total + part
    for bx in range(3):
        for by in range(3):
            spot = (where[0] + bx - 1) * counts[1] + where[1] + by - 1
            for k in range(3):
                store[(bx * 3 + by) * 3 + k] = scalar(pick(total, spot * 3 + k))


def correction(store, x, k, layout, span, depth):
    off, rows = layout
    base = lax.div(x + span, span) * 9 + k
    row = lax.broadcasted_iota(jnp.int32, (rows, depth), 0)
    high = jnp.where(row < off + 8, store[base + 3], store[base + 6])
    return jnp.where(row < off, store[base], high)


def send(msg, low, row, count):
    width = row.shape[1]
    msg[:, :, low : low + width] = jnp.broadcast_to(row.reshape(1, 1, width), (count, 1, width))


def side_rows(where, even, odd, mid):
    flip = where[1] % 2 == 1

    def wide(comp, x):
        first, second = even[comp, x], odd[comp, x]
        low = jnp.where(flip, first, second)
        high = jnp.where(flip, second, first)
        return jnp.concatenate([low, mid[comp, x], high], axis=0)

    return wide


def repack(field):
    return pltpu.roll(field, WIDE[1] - (WIDE[0] - MID[0]), 0)[: MID[1]]


def own_of(field):
    return pltpu.roll(field, MID[1] - MID[0], 0)[:8]


def center_row(moved_root, at, root, coup):
    depth = root.shape[1]
    parts = [[] for _ in range(6)]
    for low in range(0, depth, LANES):
        cut = slice(low, low + LANES)
        flat, down = [None] * 6, [None] * 6
        near = moved_root[1, at, :, cut]
        up = [coup[18 * len(HALF) + i] * near for i in range(6)]
        for q, (dx, dy) in enumerate(HALF):
            plus, minus = moved_root[dy + 1, at + dx, :, cut], moved_root[1 - dy, at - dx, :, cut]
            both, change = plus + minus, plus - minus
            for i in range(6):
                first, last = coup[q * 18 + i] * both, coup[q * 18 + 12 + i] * change
                flat[i] = first if flat[i] is None else flat[i] + first
                up[i] = up[i] + coup[q * 18 + 6 + i] * both
                down[i] = last if down[i] is None else down[i] + last
        for i in range(6):
            parts[i].append((flat[i], up[i] + down[i], up[i] - down[i]))
    total = [gather_z(one) for one in parts]
    inside = root > 0.0
    inverse = jnp.where(inside, 1.0 / jnp.where(inside, root, 1.0), 0.0)
    center = [-total[i] * inverse for i in range(6)]
    center[:3] = [one + SHIFT_MASS for one in center[:3]]
    whole = fold(center)
    half = [jnp.where(inside, SMOOTH_WEIGHT / one, 0.0) for one in whole]
    return center, half, inverse


def setup_kernel(
    dims, where, coup, even, odd, mid, cinv,
    kh_w, h_w, v_w, root_w, kh_m, h_m, v_m, root_m, kh_o, v_o, root_o, msg,
    moved_root, root_all, moved_own, sums,
):
    span, depth, devices = dims
    halo = REACH + 1
    wide = side_rows(where, even, odd, mid)

    def roots(x):
        root = jnp.sqrt(wide(3, x))
        root_all[x] = root
        shift_store(moved_root, x, [root], WIDE, WIDE)

    def diagonals(x, also_mid, also_own):
        at = x + 1
        root = root_all[at]
        center, half, inverse = center_row(moved_root, at, root, coup)
        m, o = x - (REACH - 4), x - REACH
        vectors = [wide(k, at) * inverse for k in range(3)]
        root_w[x] = root
        for k in range(3):
            h_w[k, x] = half[k]
            v_w[k, x] = vectors[k]
        for i in range(6):
            kh_w[i, x] = center[i]
        if also_mid:
            root_m[m] = repack(root)
            for k in range(3):
                h_m[k, m] = repack(half[k])
                v_m[k, m] = repack(vectors[k])
            for i in range(6):
                kh_m[i, m] = repack(center[i])
        if also_own:
            own = slice(WIDE[0], WIDE[0] + 8)
            root_o[o] = root[own]
            for k in range(3):
                v_o[k, o] = vectors[k][own]
            for i in range(6):
                kh_o[i, o] = center[i][own]

    loop(0, span + 2 * halo, roots)

    def both(also_mid, also_own):
        def body(x):
            diagonals(x, also_mid, also_own)

        return body

    edge = REACH - 4
    loop(0, edge, both(False, False))
    loop(edge, REACH, both(True, False))
    loop(REACH, REACH + span, both(True, True))
    loop(REACH + span, edge + span + 8, both(True, False))
    loop(edge + span + 8, span + 2 * REACH, both(False, False))

    def smooth(x):
        at = x + REACH - 1
        shift_store(moved_own, x, [h_w[k, at] * v_w[k, at] for k in range(3)], WIDE, OWN)

    loop(0, span + 2, smooth)

    def remain(x, carry):
        for i in (2 * x, 2 * x + 1):
            image, _ = stencil(moved_own, i + 1, coup, lambda slot, cut: kh_o[slot, i, :, cut])
            carry = tuple(carry[k] + root_o[i] * (v_o[k, i] - image[k]) for k in range(3))
        return carry

    zero = jnp.zeros((8, depth), f32)
    parts = lax.fori_loop(0, span // 2, remain, (zero, zero, zero))
    sums[...] = jnp.zeros_like(sums)
    for k in range(3):
        sums[k : k + 1] = row_sum(parts[k])
    send(msg, 0, to_lanes(sums[...]) * (1.0 / (span * 8 * depth)), devices)
    width = cinv.shape[1]
    padded = (msg.shape[2] - LANES) // 3
    for k in range(3):
        row = cinv[k : k + 1]
        if padded != width:
            row = jnp.concatenate([row, jnp.zeros((1, padded - width), f32)], axis=1)
        send(msg, LANES + k * padded, row, devices)


def iterate(dims, level, layouts, coup, store, residual, half, root, center, moved, moved_next, z_all, image):
    span, depth = dims
    source, first, second = layouts

    def begin(x):
        fields = []
        for k in range(3):
            fix = correction(store, x - level, k, source, span, depth)
            fields.append(half(k, x) * residual(k, x) + root(x) * fix)
        shift_store(moved, x, fields, source, first)

    def middle(x):
        at = x + 1
        out, near = stencil(moved, at, coup, center(at))
        fields = [near[k] + half(k, at) * (residual(k, at) - out[k]) for k in range(3)]
        for k in range(3):
            z_all[k, x] = fields[k]
        shift_store(moved_next, x, fields, first, second)

    def both(x):
        begin(x + 2)
        middle(x)

    loop(0, span + 2 * level, begin)
    loop(0, span + 2 * level - 2, middle)
    if image is not None:
        loop(0, span + 2 * level - 4, image)


def own_rows(layout):
    return slice(layout[0], layout[0] + 8)


def means_of(dims, coup, root, half, mapped, center, moved_own):
    span, depth = dims

    def begin(x):
        shift_store(moved_own, x, [half(k, x) * mapped(k, x) for k in range(3)], MID, OWN)

    def body(x, carry):
        for i in (2 * x, 2 * x + 1):
            image, _ = stencil(moved_own, i + 1, coup, lambda slot, cut: center(slot, i, cut))
            carry = tuple(carry[k] + root(i) * (own_of(mapped(k, i + 1)) - image[k]) for k in range(3))
        return carry

    loop(0, span + 2, begin)
    zero = jnp.zeros((8, depth), f32)
    return lax.fori_loop(0, span // 2, body, (zero, zero, zero))


def first_kernel(
    dims, counts, where, coup, got, kh_w, h_w, v_w, root_w, kh_m, h_m, kh_o, v_o, root_o,
    z_own, mapped, msg,
    moved, moved_next, moved_own, z_all, store, sums,
):
    span, depth, devices = dims
    level = REACH
    padded = (got.shape[2] - LANES) // 3
    coarse_values(
        got[:, 0, :LANES],
        lambda k: got[:, 0, LANES + k * padded : LANES + (k + 1) * padded],
        where, counts, store,
    )

    def image(x):
        out, _ = stencil(moved_next, x + 1, coup, lambda i, cut: kh_m[i, x, :, cut])
        for k in range(3):
            mapped[k, x] = out[k]

    iterate(
        (span, depth), level, (WIDE, WIDE, MID), coup, store,
        lambda k, x: v_w[k, x], lambda k, x: h_w[k, x], lambda x: root_w[x],
        (lambda at: lambda i, cut: kh_w[i, at, :, cut]), moved, moved_next, z_all, image,
    )
    inner = level - 2
    parts = means_of(
        (span, depth), coup, lambda x: root_o[x],
        lambda k, x: h_m[k, x + 3], lambda k, x: mapped[k, x + inner - 1],
        lambda i, x, cut: kh_o[i, x, :, cut], moved_own,
    )

    def dots(x, carry):
        gamma, delta = carry
        for k in range(3):
            z = z_all[k, x + level - 1, own_rows(WIDE)]
            z_own[k, x] = z
            gamma = gamma + v_o[k, x] * z
            delta = delta + own_of(mapped[k, x + inner]) * z
        return gamma, delta

    zero = jnp.zeros((8, depth), f32)
    gamma, delta = lax.fori_loop(0, span, dots, (zero, zero))
    scale = 1.0 / (span * 8 * depth)
    sums[...] = jnp.zeros_like(sums)
    for k in range(3):
        sums[k : k + 1] = row_sum(parts[k]) * scale
    sums[3:4] = row_sum(gamma)
    sums[4:5] = row_sum(delta)
    send(msg, 0, to_lanes(sums[...]), devices)


def second_kernel(
    dims, counts, where, coup, got, first, kh_m, h_m, v_m, root_m, kh_o, root_o, mapped_old,
    z_own, mapped, residual, means, msg,
    moved, moved_next, moved_own, z_all, store, sums,
):
    span, depth, devices = dims
    level = REACH - 2
    total = row_sum(got[:, 0])
    gamma = pick(total, 3)
    step = gamma / pick(total, 4)
    padded = (first.shape[2] - LANES) // 3
    fresh = first[:, 0, :LANES] - step * got[:, 0]
    means[...] = fresh
    coarse_values(
        fresh,
        lambda k: first[:, 0, LANES + k * padded : LANES + (k + 1) * padded],
        where, counts, store,
    )
    size = scalar(step)

    def rest(k, x):
        return v_m[k, x] - size * mapped_old[k, x]

    def image(x):
        out, _ = stencil(moved_next, x + 1, coup, lambda i, cut: kh_m[i, x + 2, :, cut])
        for k in range(3):
            mapped[k, x] = out[k]

    iterate(
        (span, depth), level, (MID, MID, MID), coup, store,
        rest, lambda k, x: h_m[k, x], lambda x: root_m[x],
        (lambda at: lambda i, cut: kh_m[i, at, :, cut]), moved, moved_next, z_all, image,
    )
    inner = level - 2
    parts = means_of(
        (span, depth), coup, lambda x: root_o[x],
        lambda k, x: h_m[k, x + 3], lambda k, x: mapped[k, x + inner - 1],
        lambda i, x, cut: kh_o[i, x, :, cut], moved_own,
    )

    def dots(x, carry):
        gamma, delta, cross = carry
        for k in range(3):
            z = own_of(z_all[k, x + level - 1])
            z_own[k, x] = z
            gamma = gamma + own_of(rest(k, x + level)) * z
            delta = delta + own_of(mapped[k, x + inner]) * z
            cross = cross + own_of(mapped_old[k, x + 4]) * z
        return gamma, delta, cross

    zero = jnp.zeros((8, depth), f32)
    dotted = lax.fori_loop(0, span, dots, (zero, zero, zero))

    def keep(x):
        for k in range(3):
            residual[k, x] = rest(k, x + inner)

    loop(0, span + 2 * inner, keep)
    scale = 1.0 / (span * 8 * depth)
    sums[...] = jnp.zeros_like(sums)
    for k in range(3):
        sums[k : k + 1] = row_sum(parts[k]) * scale
        sums[k + 3 : k + 4] = row_sum(dotted[k])
    send(msg, 0, to_lanes(sums[...]), devices)


def third_kernel(
    dims, counts, where, coup, got, got_old, first, means, kh_m, h_m, root_m, kh_o, v_o, root_o,
    z_old, mapped_old, z_new, mapped_new, residual_old, lanczos, previous, locked,
    base, z_out, dir_out, scal, msg,
    moved, moved_next, residual, mapped, z_all, store, sums, locked_sums,
):
    span, depth, devices = dims
    level = REACH - 4
    total_old = row_sum(got_old[:, 0])
    total = row_sum(got[:, 0])
    gamma_old = pick(total_old, 3)
    delta_old = pick(total_old, 4)
    step_old = gamma_old / delta_old
    gamma = pick(total, 3)
    ratio = gamma / gamma_old
    delta = pick(total, 4) + 2.0 * ratio * pick(total, 5) + ratio * ratio * delta_old
    step = gamma / delta
    fresh = means[...] - step * (got[:, 0] + ratio * got_old[:, 0])
    padded = (first.shape[2] - LANES) // 3
    coarse_values(
        fresh,
        lambda k: first[:, 0, LANES + k * padded : LANES + (k + 1) * padded],
        where, counts, store,
    )
    lane = lax.broadcasted_iota(jnp.int32, (1, LANES), 1)
    scal[...] = jnp.where(lane == 0, gamma, jnp.where(lane == 1, delta, 0.0))
    size, size_old, blend = scalar(step), scalar(step_old), scalar(ratio)

    def update(x):
        for k in range(3):
            mapped[k, x] = mapped_new[k, x] + blend * mapped_old[k, x + 2]
            residual[k, x] = residual_old[k, x] - size * mapped[k, x]

    loop(0, span + 2 * level, update)
    iterate(
        (span, depth), level, (MID, MID, OWN), coup, store,
        lambda k, x: residual[k, x], lambda k, x: h_m[k, x + 2], lambda x: root_m[x + 2],
        (lambda at: lambda i, cut: kh_m[i, at + 2, :, cut]), moved, moved_next, z_all, None,
    )

    def finish(x, carry):
        gamma, delta, cross, with_base, with_z, with_dir, weight = carry
        image, near = stencil(moved_next, x + 1, coup, lambda i, cut: kh_o[i, x, :, cut])
        inverse = 1.0 / root_o[x]
        for k in range(3):
            z = near[k]
            direction = z_new[k, x] + blend * z_old[k, x]
            partial = size_old * z_old[k, x] + size * direction
            vector = v_o[k, x]
            gamma = gamma + own_of(residual[k, x + level]) * z
            delta = delta + image[k] * z
            cross = cross + own_of(mapped[k, x + level]) * z
            with_base = with_base + vector * partial
            with_z = with_z + vector * z
            with_dir = with_dir + vector * direction
            weight = weight + lanczos[k, x] * lanczos[k, x]
            z_out[k, x] = z * inverse
            dir_out[k, x] = direction * inverse
            base[k, x] = partial * inverse - coup[18 * len(HALF) + 6] * previous[k, x]
        return gamma, delta, cross, with_base, with_z, with_dir, weight

    zero = jnp.zeros((8, depth), f32)
    dotted = lax.fori_loop(0, span, finish, (zero,) * 7)
    sums[...] = jnp.zeros_like(sums)
    for k in range(7):
        sums[k : k + 1] = row_sum(dotted[k])

    def project(n):
        def body(x, carry):
            out = list(carry)
            for k in range(3):
                vector = locked[n, k, x]
                out[0] = out[0] + vector * base[k, x]
                out[1] = out[1] + vector * z_out[k, x]
                out[2] = out[2] + vector * dir_out[k, x]
                out[3] = out[3] + vector * lanczos[k, x]
            return tuple(out)

        four = lax.fori_loop(0, span, body, (zero,) * 4, unroll=True)
        rows = [row_sum(one) for one in four]
        locked_sums[n] = jnp.concatenate(rows, axis=0)

    count = locked.shape[0]
    loop(0, count, project)
    send(msg, 0, to_lanes(sums[...]), devices)
    flat = locked_sums[...].reshape(count * 4, depth)
    send(msg, LANES, to_lanes(flat), devices)


def last_kernel(
    dims, got, scal, base, z, direction, lanczos, locked,
    remainder, weights, found, msg,
    sums,
):
    span, depth, devices = dims
    count = locked.shape[0]
    total = row_sum(got[:, 0])
    head, tail = total[:, :LANES], total[:, LANES:]
    gamma_old, delta_old = pick(scal[...], 0), pick(scal[...], 1)
    gamma = pick(head, 0)
    ratio = gamma / gamma_old
    delta = pick(head, 1) + 2.0 * ratio * pick(head, 2) + ratio * ratio * delta_old
    step = gamma / delta
    inner = pick(head, 3) + step * (pick(head, 4) + ratio * pick(head, 5))
    alpha = inner / pick(head, 6)
    lane = lax.broadcasted_iota(jnp.int32, (1, LANES), 1)
    kind = lane % 4
    factor = jnp.where(kind == 0, 1.0, jnp.where(kind == 1, step, jnp.where(kind == 2, step * ratio, -alpha)))
    terms = jnp.where(lane < 4 * count, tail * factor, 0.0)
    for n in range(count):
        value = jnp.sum(jnp.where(lane // 4 == n, terms, 0.0), axis=1, keepdims=True)
        weights[n] = scalar(value)
    found[0] = scalar(alpha)
    size, both, shrink = scalar(step), scalar(step * ratio), scalar(alpha)

    def body(x, square):
        for k in range(3):
            rest = base[k, x] + size * z[k, x] + both * direction[k, x] - shrink * lanczos[k, x]
            taken = weights[0] * locked[0, k, x]
            for n in range(1, count):
                taken = taken + weights[n] * locked[n, k, x]
            rest = rest - taken
            remainder[k, x] = rest
            square = square + rest * rest
        return square

    square = lax.fori_loop(0, span, body, jnp.zeros((8, depth), f32))
    sums[...] = jnp.zeros_like(sums)
    sums[0:1] = row_sum(square)
    send(msg, 0, to_lanes(sums[...]), devices)


def closing_kernel(cells, got, found, out):
    total = jnp.sum(row_sum(got[:, 0])[:, :8], axis=1, keepdims=True)
    out[0] = found[0]
    out[1] = scalar(jnp.sqrt(total / cells))


VMEM = pl.BlockSpec(memory_space=pltpu.VMEM)
SMEM = pl.BlockSpec(memory_space=pltpu.SMEM)


def call(kernel, name, outs, scratch, *operands, limit=60 << 20):
    return pl.pallas_call(
        kernel,
        name=name,
        out_shape=[jax.ShapeDtypeStruct(shape, f32) for shape in outs],
        in_specs=[SMEM if len(operand.shape) == 1 else VMEM for operand in operands],
        out_specs=[SMEM if len(shape) == 1 else VMEM for shape in outs],
        scratch_shapes=scratch,
        compiler_params=pltpu.CompilerParams(vmem_limit_bytes=limit),
    )(*operands)


def swap_permutes(axis):
    count = lax.axis_size(axis)
    near = [(i, i ^ 1) for i in range(count) if i ^ 1 < count]
    far = [(i, ((i + 1) ^ 1) - 1) for i in range(count)]
    return near, [(i, j) for i, j in far if 0 <= j < count]


def exchange_rows(rows):
    return lax.all_to_all(rows, AXES, 0, 0, tiled=True)


def shards(
    lanczos_vector, previous_vector, previous_beta, locked_vectors, occupancy, young, couplings, coarse_inverse
):
    _, span, span_y, depth = lanczos_vector.shape
    counts = (lax.axis_size("slab"), lax.axis_size("block"))
    devices = counts[0] * counts[1]
    locked = locked_vectors.shape[0]
    halo = REACH + 1
    assert span_y == 8 and span >= halo and locked * 4 <= LANES
    slab, block = lax.axis_index("slab"), lax.axis_index("block")
    where = jnp.stack([slab, block]).astype(jnp.int32)
    flat = -couplings.reshape(-1, 9)
    a, b, c = flat[:, 1], flat[:, 2], flat[:, 5]
    six = jnp.stack([flat[:, 0] - a - b, flat[:, 4] - a - c, flat[:, 8] - b - c, a, b, c], axis=1)
    flat, up, down = six[1:12:3], six[2:12:3], six[0:12:3]
    groups = jnp.stack([flat, 0.5 * (up + down), 0.5 * (up - down)], axis=1)
    coup = jnp.concatenate([groups.reshape(-1), six[12], previous_beta.reshape(1)])

    density = jnp.where(occupancy == 1, 1.0, VOID_DENSITY).astype(f32)
    density = jnp.repeat(jnp.repeat(jnp.repeat(density, BRICK, 0), BRICK, 1), BRICK, 2)
    stiffness = density * young
    fields = jnp.concatenate([lanczos_vector, stiffness[None]], axis=0)

    odd = slab % 2
    near, far = swap_permutes("slab")
    upper = lax.slice_in_dim(fields, span - halo, span, axis=1)
    lower = lax.slice_in_dim(fields, 0, halo, axis=1)
    from_near = lax.ppermute(jnp.where(odd == 0, upper, lower), "slab", near)
    from_far = lax.ppermute(jnp.where(odd == 0, lower, upper), "slab", far)
    below = jnp.where(odd == 0, from_far, from_near)
    above = jnp.where(odd == 0, from_near, from_far)
    tall = jnp.concatenate([below, fields, above], axis=1)
    near, far = swap_permutes("block")
    tall, where, coup, coarse_inverse = lax.optimization_barrier((tall, where, coup, coarse_inverse))
    side_near = lax.ppermute(tall, "block", near)
    side_far = lax.ppermute(tall, "block", far)

    dims = (span, depth, devices)
    wide = (span + 2 * REACH, WIDE[1], depth)
    mid = (span + 8, MID[1], depth)
    own = (3, span, 8, depth)
    padded = -(-coarse_inverse.shape[1] // LANES) * LANES
    row = (devices, 1, LANES)

    def scratch(*shape):
        return pltpu.VMEM(shape, f32)

    kh_w, h_w, v_w, root_w, kh_m, h_m, v_m, root_m, kh_o, v_o, root_o, msg = call(
        functools.partial(setup_kernel, dims),
        "setup",
        [
            (6, *wide), (3, *wide), (3, *wide), wide, (6, *mid), (3, *mid), (3, *mid), mid,
            (6, *own[1:]), own, own[1:], (devices, 1, LANES + 3 * padded),
        ],
        [
            scratch(3, span + 2 * halo + 1, WIDE[1], depth),
            scratch(span + 2 * halo + 1, WIDE[1], depth),
            scratch(9, span + 2, 8, depth),
            scratch(8, depth),
        ],
        where, coup, side_near, side_far, tall, coarse_inverse, limit=9 << 20,
    )
    first = exchange_rows(msg)

    store = pltpu.SMEM((27,), f32)
    z_0, mapped_0, msg = call(
        functools.partial(first_kernel, dims, counts),
        "first",
        [own, (3, *mid), row],
        [
            scratch(9, *wide),
            scratch(9, span + 2 * REACH - 2, MID[1], depth),
            scratch(9, span + 2, 8, depth),
            scratch(3, span + 2 * REACH - 2, WIDE[1], depth),
            store,
            scratch(8, depth),
        ],
        where, coup, first, kh_w, h_w, v_w, root_w, kh_m, h_m, kh_o, v_o, root_o, limit=28 << 20,
    )
    got_0 = exchange_rows(msg)

    level = REACH - 2
    inner = (3, span + 2 * level - 4, MID[1], depth)
    z_1, mapped_1, residual, means, msg = call(
        functools.partial(second_kernel, dims, counts),
        "second",
        [own, inner, inner, (devices, LANES), row],
        [
            scratch(9, *mid),
            scratch(9, span + 2 * level - 2, MID[1], depth),
            scratch(9, span + 2, 8, depth),
            scratch(3, span + 2 * level - 2, MID[1], depth),
            store,
            scratch(8, depth),
        ],
        where, coup, got_0, first, kh_m, h_m, v_m, root_m, kh_o, root_o, mapped_0, limit=18 << 20,
    )
    got_1 = exchange_rows(msg)

    level = REACH - 4
    base, z_2, direction, scal, msg = call(
        functools.partial(third_kernel, dims, counts),
        "third",
        [own, own, own, (1, LANES), (devices, 1, 2 * LANES)],
        [
            scratch(9, span + 2 * level, MID[1], depth),
            scratch(9, span + 2 * level - 2, 8, depth),
            scratch(3, span + 2 * level, MID[1], depth),
            scratch(3, span + 2 * level, MID[1], depth),
            scratch(3, span + 2 * level - 2, MID[1], depth),
            store,
            scratch(8, depth),
            scratch(locked, 4, depth),
        ],
        where, coup, got_1, got_0, first, means, kh_m, h_m, root_m, kh_o, v_o, root_o,
        z_0, mapped_0, z_1, mapped_1, residual, lanczos_vector, previous_vector, locked_vectors, limit=16 << 20,
    )
    got_2 = exchange_rows(msg)

    remainder, projections, found, msg = call(
        functools.partial(last_kernel, dims),
        "last",
        [own, (locked,), (1,), row],
        [scratch(8, depth)],
        got_2, scal, base, z_2, direction, lanczos_vector, locked_vectors, limit=6 << 20,
    )
    (coefficients,) = call(
        functools.partial(closing_kernel, 3.0 * span * span_y * depth * devices),
        "closing",
        [(2,)],
        [],
        exchange_rows(msg), found, limit=4 << 20,
    )
    return remainder, coefficients, projections


def solution(mesh):
    in_specs = (
        P(None, "slab", "block", None),
        P(None, "slab", "block", None),
        P(),
        P(None, None, "slab", "block", None),
        P("slab", "block", None),
        P("slab", "block", None),
        P(),
        P(("slab", "block"), None),
    )
    out_specs = (P(None, "slab", "block", None), P(), P())
    return jax.shard_map(shards, mesh=mesh, in_specs=in_specs, out_specs=out_specs, check_vma=False)
```

```python
import functools

import jax
import jax.numpy as jnp
from jax import lax
from jax.experimental import pallas as pl
from jax.experimental.pallas import tpu as pltpu
from jax.sharding import PartitionSpec as P

BRICK = 8
ITERS = 3
SHIFT_MASS = 0.02
SMOOTH_WEIGHT = 0.5
VOID_DENSITY = 0.1

AXES = ("slab", "block")
LANES = 128
WIDE = (8, 24)
MID = (4, 16)
OWN = (0, 8)
REACH = 2 * ITERS
HALF = [(-1, -1), (-1, 0), (-1, 1), (0, -1)]
f32 = jnp.float32


def along_z(chunks, dz):
    lane = lax.broadcasted_iota(jnp.int32, chunks[0].shape, 1)
    turned = [pltpu.roll(chunk, (-dz) % LANES, 1) for chunk in chunks]
    edge = 0 if dz < 0 else LANES - 1
    out = []
    for number, chunk in enumerate(turned):
        other = number + dz
        filler = turned[other] if 0 <= other < len(turned) else 0.0
        out.append(jnp.where(lane == edge, filler, chunk))
    return out


def shift_store(dest, at, fields, source, target):
    src_off, src_rows = source
    dst_off, dst_rows = target
    for comp, field in enumerate(fields):
        for dy in (-1, 0, 1):
            shift = src_off - dst_off + dy
            moved = field if shift == 0 else pltpu.roll(field, (-shift) % src_rows, 0)
            if dst_rows != src_rows:
                moved = moved[:dst_rows]
            dest[(dy + 1) * len(fields) + comp, at] = moved


def gather_z(parts):
    flat, up, down = zip(*parts)
    above, below = along_z(up, 1), along_z(down, -1)
    return jnp.concatenate([a + (b + c) for a, b, c in zip(flat, above, below)], axis=1)


def stencil(moved, at, coup, center):
    depth = moved.shape[3]
    parts = [[], [], []]
    rows = []
    for low in range(0, depth, LANES):
        cut = slice(low, low + LANES)
        near = [moved[3 + c, at, :, cut] for c in range(3)]
        rows.append(near)
        flat, up, down = [], [], [None] * 6
        for i, value in enumerate(six_of(near)):
            flat.append(center(i, cut) * value)
            up.append(coup[18 * len(HALF) + i] * value)
        for q, (dx, dy) in enumerate(HALF):
            plus = [moved[(dy + 1) * 3 + c, at + dx, :, cut] for c in range(3)]
            minus = [moved[(1 - dy) * 3 + c, at - dx, :, cut] for c in range(3)]
            for i, value in enumerate(six_of([p + m for p, m in zip(plus, minus)])):
                flat[i] = flat[i] + coup[q * 18 + i] * value
                up[i] = up[i] + coup[q * 18 + 6 + i] * value
            for i, value in enumerate(six_of([p - m for p, m in zip(plus, minus)])):
                term = coup[q * 18 + 12 + i] * value
                down[i] = term if down[i] is None else down[i] + term
        flat, up, down = fold(flat), fold(up), fold(down)
        for k in range(3):
            parts[k].append((flat[k], up[k] + down[k], up[k] - down[k]))
    near = [jnp.concatenate([row[k] for row in rows], axis=1) for k in range(3)]
    return [gather_z(one) for one in parts], near


def fold(six):
    return [six[0] + (six[3] + six[4]), six[1] + (six[3] + six[5]), six[2] + (six[4] + six[5])]


def six_of(three):
    return [*three, three[0] + three[1], three[0] + three[2], three[1] + three[2]]


def loop(low, high, body):
    def step(i, carry):
        body(i)
        return carry

    lax.fori_loop(low, high, step, 0)


def row_sum(x):
    return jnp.sum(x, axis=0, keepdims=True)


def to_lanes(rows):
    column = jnp.sum(rows, axis=1, keepdims=True)
    count = rows.shape[0]
    here = lax.broadcasted_iota(jnp.int32, (count, LANES), 0)
    lane = lax.broadcasted_iota(jnp.int32, (count, LANES), 1)
    return row_sum(jnp.where(here == lane, column, 0.0))


def pick(row, index):
    lane = lax.broadcasted_iota(jnp.int32, row.shape, 1)
    return jnp.sum(jnp.where(lane == index, row, 0.0), axis=1, keepdims=True)


def scalar(one):
    return one[0, 0]


def coarse_values(means, rows, store):
    shape = (means.shape[0], rows.shape[1])
    row = lax.broadcasted_iota(jnp.int32, shape, 0)
    lane = lax.broadcasted_iota(jnp.int32, shape, 1)
    spread = jnp.zeros(shape, f32)
    for k in range(3):
        spread = jnp.where(lane == 3 * row + k, means[:, k : k + 1], spread)
    column = jnp.sum(rows[...] * row_sum(spread), axis=1, keepdims=True)
    for slot in range(27):
        store[slot] = column[slot, 0]


def correction(store, x, k, layout, span, depth):
    off, rows = layout
    base = lax.div(x + span, span) * 9 + k
    row = lax.broadcasted_iota(jnp.int32, (rows, depth), 0)
    high = jnp.where(row < off + 8, store[base + 3], store[base + 6])
    return jnp.where(row < off, store[base], high)


def send(msg, low, row, count):
    width = row.shape[1]
    msg[:, :, low : low + width] = jnp.broadcast_to(row.reshape(1, 1, width), (count, 1, width))


def pack_kernel(
    dims, where, occupancy, vector_in, young_in, cinv_in,
    near, far, vector, stiff, coarse,
    young, cinv, sems,
):
    span, depth, _ = dims
    copies = [
        pltpu.make_async_copy(source, target, sems.at[number])
        for number, (source, target) in enumerate([(young_in, young), (cinv_in, cinv), (vector_in, vector)])
    ]
    for copy in copies:
        copy.start()
    lane = lax.broadcasted_iota(jnp.int32, (8, depth), 1)
    density = jnp.full((8, depth), VOID_DENSITY, f32)
    for brick in range(depth // BRICK):
        solid = jnp.where(occupancy[brick] == 1, 1.0, VOID_DENSITY).astype(f32)
        density = jnp.where(lane // BRICK == brick, solid, density)
    for copy in copies:
        copy.wait()
    for x in range(span):
        stiff[x] = density * young[x]
    width = cinv.shape[1]
    coarse[...] = jnp.zeros_like(coarse)
    for t in range(coarse.shape[0]):
        count = min(depth, width - t * depth)
        coarse[t, 0:3, 0:count] = cinv[:, t * depth : t * depth + count]
    flip = where[0] % 2 == 1
    halo = REACH + 1

    def put(tile, low, high):
        near[tile] = jnp.where(flip, low, high)
        far[tile] = jnp.where(flip, high, low)

    for k in range(3):
        for j in range(REACH):
            put(k * REACH + j, vector[k, j], vector[k, span - REACH + j])
    for j in range(halo):
        put(3 * REACH + j, stiff[j], stiff[span - halo + j])
    for t in range(coarse.shape[0]):
        put(3 * REACH + halo + t, coarse[t], coarse[t])


def tall_kernel(dims, where, near, far, vector, stiff, coarse, tall):
    span, _, _ = dims
    halo = REACH + 1
    flip = where[0] % 2 == 1

    def sides(tile):
        first, second = near[tile], far[tile]
        return jnp.where(flip, first, second), jnp.where(flip, second, first)

    for k in range(3):
        base = k * (span + 2 * REACH)
        for j in range(REACH):
            tall[base + j], tall[base + REACH + span + j] = sides(k * REACH + j)
        for x in range(span):
            tall[base + REACH + x] = vector[k, x]
    base = 3 * (span + 2 * REACH)
    for j in range(halo):
        tall[base + j], tall[base + halo + span + j] = sides(3 * REACH + j)
    for x in range(span):
        tall[base + halo + x] = stiff[x]
    base, pieces = base + span + 2 * halo, coarse.shape[0]
    for t in range(pieces):
        tall[base + t], tall[base + 2 * pieces + t] = sides(3 * REACH + halo + t)
        tall[base + pieces + t] = coarse[t]


def side_tiles(where, even, odd, mid):
    flip = where[1] % 2 == 1

    def three(tile):
        first, second = even[tile], odd[tile]
        return jnp.where(flip, first, second), mid[tile], jnp.where(flip, second, first)

    return three


def repack(field):
    return pltpu.roll(field, WIDE[1] - (WIDE[0] - MID[0]), 0)[: MID[1]]


def own_of(field):
    return pltpu.roll(field, MID[1] - MID[0], 0)[:8]


def center_row(moved_root, at, root, coup):
    depth = root.shape[1]
    parts = [[] for _ in range(6)]
    for low in range(0, depth, LANES):
        cut = slice(low, low + LANES)
        flat, down = [None] * 6, [None] * 6
        near = moved_root[1, at, :, cut]
        up = [coup[18 * len(HALF) + i] * near for i in range(6)]
        for q, (dx, dy) in enumerate(HALF):
            plus, minus = moved_root[dy + 1, at + dx, :, cut], moved_root[1 - dy, at - dx, :, cut]
            both, change = plus + minus, plus - minus
            for i in range(6):
                first, last = coup[q * 18 + i] * both, coup[q * 18 + 12 + i] * change
                flat[i] = first if flat[i] is None else flat[i] + first
                up[i] = up[i] + coup[q * 18 + 6 + i] * both
                down[i] = last if down[i] is None else down[i] + last
        for i in range(6):
            parts[i].append((flat[i], up[i] + down[i], up[i] - down[i]))
    total = [gather_z(one) for one in parts]
    inside = root > 0.0
    inverse = jnp.where(inside, 1.0 / jnp.where(inside, root, 1.0), 0.0)
    center = [-total[i] * inverse for i in range(6)]
    center[:3] = [one + SHIFT_MASS for one in center[:3]]
    whole = fold(center)
    half = [jnp.where(inside, SMOOTH_WEIGHT / one, 0.0) for one in whole]
    return center, half, inverse


def setup_kernel(
    dims, where, coup, even, odd, mid,
    kh_w, h_w, v_w, root_w, kh_m, h_m, v_m, root_m, kh_o, v_o, root_o, coarse_rows, msg,
    moved_root, root_all, moved_own, sums,
):
    span, depth, devices = dims
    halo = REACH + 1
    three = side_tiles(where, even, odd, mid)
    count = span + 2 * REACH

    def wide(tile):
        return jnp.concatenate(three(tile), axis=0)


    def roots(x):
        root = jnp.sqrt(wide(3 * count + x))
        root_all[x] = root
        shift_store(moved_root, x, [root], WIDE, WIDE)

    def diagonals(x, also_mid, also_own):
        at = x + 1
        root = root_all[at]
        center, half, inverse = center_row(moved_root, at, root, coup)
        m, o = x - (REACH - 4), x - REACH
        vectors = [wide(k * count + x) * inverse for k in range(3)]
        root_w[x] = root
        for k in range(3):
            h_w[k, x] = half[k]
            v_w[k, x] = vectors[k]
        for i in range(6):
            kh_w[i, x] = center[i]
        if also_mid:
            root_m[m] = repack(root)
            for k in range(3):
                h_m[k, m] = repack(half[k])
                v_m[k, m] = repack(vectors[k])
            for i in range(6):
                kh_m[i, m] = repack(center[i])
        if also_own:
            own = slice(WIDE[0], WIDE[0] + 8)
            root_o[o] = root[own]
            for k in range(3):
                v_o[k, o] = vectors[k][own]
            for i in range(6):
                kh_o[i, o] = center[i][own]

    loop(0, span + 2 * halo, roots)

    def both(also_mid, also_own):
        def body(x):
            diagonals(x, also_mid, also_own)

        return body

    edge = REACH - 4
    loop(0, edge, both(False, False))
    loop(edge, REACH, both(True, False))
    loop(REACH, REACH + span, both(True, True))
    loop(REACH + span, edge + span + 8, both(True, False))
    loop(edge + span + 8, span + 2 * REACH, both(False, False))

    def smooth(x):
        at = x + REACH - 1
        shift_store(moved_own, x, [h_w[k, at] * v_w[k, at] for k in range(3)], WIDE, OWN)

    loop(0, span + 2, smooth)

    def remain(x, carry):
        for i in (2 * x, 2 * x + 1):
            image, _ = stencil(moved_own, i + 1, coup, lambda slot, cut: kh_o[slot, i, :, cut])
            carry = tuple(carry[k] + root_o[i] * (v_o[k, i] - image[k]) for k in range(3))
        return carry

    zero = jnp.zeros((8, depth), f32)
    parts = lax.fori_loop(0, span // 2, remain, (zero, zero, zero))
    sums[...] = jnp.zeros_like(sums)
    for k in range(3):
        sums[k : k + 1] = row_sum(parts[k])
    send(msg, 0, to_lanes(sums[...]) * (1.0 / (span * 8 * depth)), devices)
    base = 3 * count + span + 2 * halo
    pieces = coarse_rows.shape[1] // depth
    coarse_rows[...] = jnp.zeros_like(coarse_rows)
    for bx in range(3):
        for t in range(pieces):
            for by, tile in enumerate(three(base + bx * pieces + t)):
                low = (bx * 3 + by) * 3
                coarse_rows[low : low + 3, t * depth : (t + 1) * depth] = tile[:3]


def iterate(dims, level, layouts, coup, store, residual, half, root, center, moved, moved_next, z_all, image):
    span, depth = dims
    source, first, second = layouts

    def begin(x):
        fields = []
        for k in range(3):
            fix = correction(store, x - level, k, source, span, depth)
            fields.append(half(k, x) * residual(k, x) + root(x) * fix)
        shift_store(moved, x, fields, source, first)

    def middle(x):
        at = x + 1
        out, near = stencil(moved, at, coup, center(at))
        fields = [near[k] + half(k, at) * (residual(k, at) - out[k]) for k in range(3)]
        for k in range(3):
            z_all[k, x] = fields[k]
        shift_store(moved_next, x, fields, first, second)

    def both(x):
        begin(x + 2)
        middle(x)

    loop(0, span + 2 * level, begin)
    loop(0, span + 2 * level - 2, middle)
    if image is not None:
        loop(0, span + 2 * level - 4, image)


def own_rows(layout):
    return slice(layout[0], layout[0] + 8)


def means_of(dims, coup, root, half, mapped, center, moved_own):
    span, depth = dims

    def begin(x):
        shift_store(moved_own, x, [half(k, x) * mapped(k, x) for k in range(3)], MID, OWN)

    def body(x, carry):
        for i in (2 * x, 2 * x + 1):
            image, _ = stencil(moved_own, i + 1, coup, lambda slot, cut: center(slot, i, cut))
            carry = tuple(carry[k] + root(i) * (own_of(mapped(k, i + 1)) - image[k]) for k in range(3))
        return carry

    loop(0, span + 2, begin)
    zero = jnp.zeros((8, depth), f32)
    return lax.fori_loop(0, span // 2, body, (zero, zero, zero))


def first_kernel(
    dims, coup, got, coarse_rows, kh_w, h_w, v_w, root_w, kh_m, h_m, kh_o, v_o, root_o,
    z_own, mapped, msg,
    moved, moved_next, moved_own, z_all, store, sums,
):
    span, depth, devices = dims
    level = REACH
    coarse_values(got[:, 0], coarse_rows, store)

    def image(x):
        out, _ = stencil(moved_next, x + 1, coup, lambda i, cut: kh_m[i, x, :, cut])
        for k in range(3):
            mapped[k, x] = out[k]

    iterate(
        (span, depth), level, (WIDE, WIDE, MID), coup, store,
        lambda k, x: v_w[k, x], lambda k, x: h_w[k, x], lambda x: root_w[x],
        (lambda at: lambda i, cut: kh_w[i, at, :, cut]), moved, moved_next, z_all, image,
    )
    inner = level - 2
    parts = means_of(
        (span, depth), coup, lambda x: root_o[x],
        lambda k, x: h_m[k, x + 3], lambda k, x: mapped[k, x + inner - 1],
        lambda i, x, cut: kh_o[i, x, :, cut], moved_own,
    )

    def dots(x, carry):
        gamma, delta = carry
        for k in range(3):
            z = z_all[k, x + level - 1, own_rows(WIDE)]
            z_own[k, x] = z
            gamma = gamma + v_o[k, x] * z
            delta = delta + own_of(mapped[k, x + inner]) * z
        return gamma, delta

    zero = jnp.zeros((8, depth), f32)
    gamma, delta = lax.fori_loop(0, span, dots, (zero, zero))
    scale = 1.0 / (span * 8 * depth)
    sums[...] = jnp.zeros_like(sums)
    for k in range(3):
        sums[k : k + 1] = row_sum(parts[k]) * scale
    sums[3:4] = row_sum(gamma)
    sums[4:5] = row_sum(delta)
    send(msg, 0, to_lanes(sums[...]), devices)


def second_kernel(
    dims, coup, got, first, coarse_rows, kh_m, h_m, v_m, root_m, kh_o, root_o, mapped_old,
    z_own, mapped, residual, means, msg,
    moved, moved_next, moved_own, z_all, store, sums,
):
    span, depth, devices = dims
    level = REACH - 2
    total = row_sum(got[:, 0])
    gamma = pick(total, 3)
    step = gamma / pick(total, 4)
    fresh = first[:, 0] - step * got[:, 0]
    means[...] = fresh
    coarse_values(fresh, coarse_rows, store)
    size = scalar(step)

    def rest(k, x):
        return v_m[k, x] - size * mapped_old[k, x]

    def image(x):
        out, _ = stencil(moved_next, x + 1, coup, lambda i, cut: kh_m[i, x + 2, :, cut])
        for k in range(3):
            mapped[k, x] = out[k]

    iterate(
        (span, depth), level, (MID, MID, MID), coup, store,
        rest, lambda k, x: h_m[k, x], lambda x: root_m[x],
        (lambda at: lambda i, cut: kh_m[i, at, :, cut]), moved, moved_next, z_all, image,
    )
    inner = level - 2
    parts = means_of(
        (span, depth), coup, lambda x: root_o[x],
        lambda k, x: h_m[k, x + 3], lambda k, x: mapped[k, x + inner - 1],
        lambda i, x, cut: kh_o[i, x, :, cut], moved_own,
    )

    def dots(x, carry):
        gamma, delta, cross = carry
        for k in range(3):
            z = own_of(z_all[k, x + level - 1])
            z_own[k, x] = z
            gamma = gamma + own_of(rest(k, x + level)) * z
            delta = delta + own_of(mapped[k, x + inner]) * z
            cross = cross + own_of(mapped_old[k, x + 4]) * z
        return gamma, delta, cross

    zero = jnp.zeros((8, depth), f32)
    dotted = lax.fori_loop(0, span, dots, (zero, zero, zero))

    def keep(x):
        for k in range(3):
            residual[k, x] = rest(k, x + inner)

    loop(0, span + 2 * inner, keep)
    scale = 1.0 / (span * 8 * depth)
    sums[...] = jnp.zeros_like(sums)
    for k in range(3):
        sums[k : k + 1] = row_sum(parts[k]) * scale
        sums[k + 3 : k + 4] = row_sum(dotted[k])
    send(msg, 0, to_lanes(sums[...]), devices)


def third_kernel(
    dims, coup, got, got_old, means, coarse_rows, kh_m, h_m, root_m, kh_o, v_o, root_o,
    z_old, mapped_old, z_new, mapped_new, residual_old, lanczos, previous, locked,
    base, z_out, dir_out, scal, msg,
    moved, moved_next, residual, mapped, z_all, store, sums, locked_sums,
):
    span, depth, devices = dims
    level = REACH - 4
    total_old = row_sum(got_old[:, 0])
    total = row_sum(got[:, 0])
    gamma_old = pick(total_old, 3)
    delta_old = pick(total_old, 4)
    step_old = gamma_old / delta_old
    gamma = pick(total, 3)
    ratio = gamma / gamma_old
    delta = pick(total, 4) + 2.0 * ratio * pick(total, 5) + ratio * ratio * delta_old
    step = gamma / delta
    fresh = means[...] - step * (got[:, 0] + ratio * got_old[:, 0])
    coarse_values(fresh, coarse_rows, store)
    lane = lax.broadcasted_iota(jnp.int32, (1, LANES), 1)
    scal[...] = jnp.where(lane == 0, gamma, jnp.where(lane == 1, delta, 0.0))
    size, size_old, blend = scalar(step), scalar(step_old), scalar(ratio)

    def update(x):
        for k in range(3):
            mapped[k, x] = mapped_new[k, x] + blend * mapped_old[k, x + 2]
            residual[k, x] = residual_old[k, x] - size * mapped[k, x]

    loop(0, span + 2 * level, update)
    iterate(
        (span, depth), level, (MID, MID, OWN), coup, store,
        lambda k, x: residual[k, x], lambda k, x: h_m[k, x + 2], lambda x: root_m[x + 2],
        (lambda at: lambda i, cut: kh_m[i, at + 2, :, cut]), moved, moved_next, z_all, None,
    )

    def finish(x, carry):
        gamma, delta, cross, with_base, with_z, with_dir, weight = carry
        image, near = stencil(moved_next, x + 1, coup, lambda i, cut: kh_o[i, x, :, cut])
        inverse = 1.0 / root_o[x]
        for k in range(3):
            z = near[k]
            direction = z_new[k, x] + blend * z_old[k, x]
            partial = size_old * z_old[k, x] + size * direction
            vector = v_o[k, x]
            gamma = gamma + own_of(residual[k, x + level]) * z
            delta = delta + image[k] * z
            cross = cross + own_of(mapped[k, x + level]) * z
            with_base = with_base + vector * partial
            with_z = with_z + vector * z
            with_dir = with_dir + vector * direction
            weight = weight + lanczos[k, x] * lanczos[k, x]
            z_out[k, x] = z * inverse
            dir_out[k, x] = direction * inverse
            base[k, x] = partial * inverse - coup[18 * len(HALF) + 6] * previous[k, x]
        return gamma, delta, cross, with_base, with_z, with_dir, weight

    zero = jnp.zeros((8, depth), f32)
    dotted = lax.fori_loop(0, span, finish, (zero,) * 7)
    sums[...] = jnp.zeros_like(sums)
    for k in range(7):
        sums[k : k + 1] = row_sum(dotted[k])

    def project(n):
        def body(x, carry):
            out = list(carry)
            for k in range(3):
                vector = locked[n, k, x]
                out[0] = out[0] + vector * base[k, x]
                out[1] = out[1] + vector * z_out[k, x]
                out[2] = out[2] + vector * dir_out[k, x]
                out[3] = out[3] + vector * lanczos[k, x]
            return tuple(out)

        four = lax.fori_loop(0, span, body, (zero,) * 4, unroll=True)
        rows = [row_sum(one) for one in four]
        locked_sums[n] = jnp.concatenate(rows, axis=0)

    count = locked.shape[0]
    loop(0, count, project)
    send(msg, 0, to_lanes(sums[...]), devices)
    flat = locked_sums[...].reshape(count * 4, depth)
    send(msg, LANES, to_lanes(flat), devices)


def last_kernel(
    dims, got, scal, base, z, direction, lanczos, locked,
    remainder, weights, found, msg,
    sums,
):
    span, depth, devices = dims
    count = locked.shape[0]
    total = row_sum(got[:, 0])
    head, tail = total[:, :LANES], total[:, LANES:]
    gamma_old, delta_old = pick(scal[...], 0), pick(scal[...], 1)
    gamma = pick(head, 0)
    ratio = gamma / gamma_old
    delta = pick(head, 1) + 2.0 * ratio * pick(head, 2) + ratio * ratio * delta_old
    step = gamma / delta
    inner = pick(head, 3) + step * (pick(head, 4) + ratio * pick(head, 5))
    alpha = inner / pick(head, 6)
    lane = lax.broadcasted_iota(jnp.int32, (1, LANES), 1)
    kind = lane % 4
    factor = jnp.where(kind == 0, 1.0, jnp.where(kind == 1, step, jnp.where(kind == 2, step * ratio, -alpha)))
    terms = jnp.where(lane < 4 * count, tail * factor, 0.0)
    for n in range(count):
        value = jnp.sum(jnp.where(lane // 4 == n, terms, 0.0), axis=1, keepdims=True)
        weights[n] = scalar(value)
    found[0] = scalar(alpha)
    size, both, shrink = scalar(step), scalar(step * ratio), scalar(alpha)

    def body(x, square):
        for k in range(3):
            rest = base[k, x] + size * z[k, x] + both * direction[k, x] - shrink * lanczos[k, x]
            taken = weights[0] * locked[0, k, x]
            for n in range(1, count):
                taken = taken + weights[n] * locked[n, k, x]
            rest = rest - taken
            remainder[k, x] = rest
            square = square + rest * rest
        return square

    square = lax.fori_loop(0, span, body, jnp.zeros((8, depth), f32))
    sums[...] = jnp.zeros_like(sums)
    sums[0:1] = row_sum(square)
    send(msg, 0, to_lanes(sums[...]), devices)


def closing_kernel(cells, got, found, out):
    total = jnp.sum(row_sum(got[:, 0])[:, :8], axis=1, keepdims=True)
    out[0] = found[0]
    out[1] = scalar(jnp.sqrt(total / cells))


VMEM = pl.BlockSpec(memory_space=pltpu.VMEM)
SMEM = pl.BlockSpec(memory_space=pltpu.SMEM)
HBM = pl.BlockSpec(memory_space=pltpu.HBM)


def call(kernel, name, outs, scratch, *operands, limit, stay=0):
    places = [SMEM if len(operand.shape) == 1 else VMEM for operand in operands]
    if stay:
        places[-stay:] = [HBM] * stay
        kept = [pltpu.with_memory_space_constraint(operand, pltpu.HBM) for operand in operands[-stay:]]
        operands = (*operands[:-stay], *kept)
    return pl.pallas_call(
        kernel,
        name=name,
        out_shape=[jax.ShapeDtypeStruct(shape, f32) for shape in outs],
        in_specs=places,
        out_specs=[SMEM if len(shape) == 1 else VMEM for shape in outs],
        scratch_shapes=scratch,
        compiler_params=pltpu.CompilerParams(vmem_limit_bytes=limit),
    )(*operands)


def swap_permutes(axis):
    count = lax.axis_size(axis)
    near = [(i, i ^ 1) for i in range(count) if i ^ 1 < count]
    far = [(i, ((i + 1) ^ 1) - 1) for i in range(count)]
    return near, [(i, j) for i, j in far if 0 <= j < count]


def exchange_rows(rows):
    return lax.all_to_all(rows, AXES, 0, 0, tiled=True)


def shards(
    lanczos_vector, previous_vector, previous_beta, locked_vectors, occupancy, young, couplings, coarse_inverse
):
    _, span, span_y, depth = lanczos_vector.shape
    counts = (lax.axis_size("slab"), lax.axis_size("block"))
    devices = counts[0] * counts[1]
    locked = locked_vectors.shape[0]
    halo = REACH + 1
    assert span_y == 8 and span >= halo and locked * 4 <= LANES
    slab, block = lax.axis_index("slab"), lax.axis_index("block")
    where = jnp.stack([slab, block]).astype(jnp.int32)
    flat = -couplings.reshape(-1, 9)
    a, b, c = flat[:, 1], flat[:, 2], flat[:, 5]
    six = jnp.stack([flat[:, 0] - a - b, flat[:, 4] - a - c, flat[:, 8] - b - c, a, b, c], axis=1)
    flat, up, down = six[1:12:3], six[2:12:3], six[0:12:3]
    groups = jnp.stack([flat, 0.5 * (up + down), 0.5 * (up - down)], axis=1)
    coup = jnp.concatenate([groups.reshape(-1), six[12], previous_beta.reshape(1)])

    dims = (span, depth, devices)
    pieces = -(-coarse_inverse.shape[1] // depth)
    own = (3, span, 8, depth)

    def scratch(*shape):
        return pltpu.VMEM(shape, f32)

    tiles = (3 * REACH + halo + pieces, 8, depth)
    near, far, vector, stiff, coarse = call(
        functools.partial(pack_kernel, dims),
        "pack",
        [tiles, tiles, own, own[1:], (pieces, 8, depth)],
        [scratch(*own[1:]), scratch(*coarse_inverse.shape), pltpu.SemaphoreType.DMA((3,))],
        where, pltpu.with_memory_space_constraint(occupancy.reshape(-1), pltpu.HBM), lanczos_vector, young, coarse_inverse, limit=6 << 20, stay=3,
    )
    to_near, to_far = swap_permutes("slab")
    near, far = lax.ppermute(near, "slab", to_near), lax.ppermute(far, "slab", to_far)
    (tall,) = call(
        functools.partial(tall_kernel, dims),
        "tall",
        [(3 * (span + 2 * REACH) + span + 2 * halo + 3 * pieces, 8, depth)],
        [],
        where, near, far, vector, stiff, coarse, limit=6 << 20,
    )
    to_near, to_far = swap_permutes("block")
    tall, coup = lax.optimization_barrier((tall, coup))
    side_near, side_far = lax.ppermute(tall, "block", to_near), lax.ppermute(tall, "block", to_far)

    wide = (span + 2 * REACH, WIDE[1], depth)
    mid = (span + 8, MID[1], depth)
    row = (devices, 1, LANES)
    kh_w, h_w, v_w, root_w, kh_m, h_m, v_m, root_m, kh_o, v_o, root_o, rows, msg = call(
        functools.partial(setup_kernel, dims),
        "setup",
        [
            (6, *wide), (3, *wide), (3, *wide), wide, (6, *mid), (3, *mid), (3, *mid), mid,
            (6, *own[1:]), own, own[1:], (32, pieces * depth), row,
        ],
        [
            scratch(3, span + 2 * halo + 1, WIDE[1], depth),
            scratch(span + 2 * halo + 1, WIDE[1], depth),
            scratch(9, span + 2, 8, depth),
            scratch(8, depth),
        ],
        where, coup, side_near, side_far, tall, limit=9 << 20,
    )
    first = exchange_rows(msg)

    store = pltpu.SMEM((27,), f32)
    z_0, mapped_0, msg = call(
        functools.partial(first_kernel, dims),
        "first",
        [own, (3, *mid), row],
        [
            scratch(9, *wide),
            scratch(9, span + 2 * REACH - 2, MID[1], depth),
            scratch(9, span + 2, 8, depth),
            scratch(3, span + 2 * REACH - 2, WIDE[1], depth),
            store,
            scratch(8, depth),
        ],
        coup, first, rows, kh_w, h_w, v_w, root_w, kh_m, h_m, kh_o, v_o, root_o, limit=14 << 20,
    )
    got_0 = exchange_rows(msg)

    level = REACH - 2
    inner = (3, span + 2 * level - 4, MID[1], depth)
    z_1, mapped_1, residual, means, msg = call(
        functools.partial(second_kernel, dims),
        "second",
        [own, inner, inner, (devices, LANES), row],
        [
            scratch(9, *mid),
            scratch(9, span + 2 * level - 2, MID[1], depth),
            scratch(9, span + 2, 8, depth),
            scratch(3, span + 2 * level - 2, MID[1], depth),
            store,
            scratch(8, depth),
        ],
        coup, got_0, first, rows, kh_m, h_m, v_m, root_m, kh_o, root_o, mapped_0, limit=10 << 20,
    )
    got_1 = exchange_rows(msg)

    level = REACH - 4
    base, z_2, direction, scal, msg = call(
        functools.partial(third_kernel, dims),
        "third",
        [own, own, own, (1, LANES), (devices, 1, 2 * LANES)],
        [
            scratch(9, span + 2 * level, MID[1], depth),
            scratch(9, span + 2 * level - 2, 8, depth),
            scratch(3, span + 2 * level, MID[1], depth),
            scratch(3, span + 2 * level, MID[1], depth),
            scratch(3, span + 2 * level - 2, MID[1], depth),
            store,
            scratch(8, depth),
            scratch(locked, 4, depth),
        ],
        coup, got_1, got_0, means, rows, kh_m, h_m, root_m, kh_o, v_o, root_o,
        z_0, mapped_0, z_1, mapped_1, residual, lanczos_vector, previous_vector, locked_vectors, limit=9 << 20,
    )
    got_2 = exchange_rows(msg)

    remainder, projections, found, msg = call(
        functools.partial(last_kernel, dims),
        "last",
        [own, (locked,), (1,), row],
        [scratch(8, depth)],
        got_2, scal, base, z_2, direction, lanczos_vector, locked_vectors, limit=6 << 20,
    )
    (coefficients,) = call(
        functools.partial(closing_kernel, 3.0 * span * span_y * depth * devices),
        "closing",
        [(2,)],
        [],
        exchange_rows(msg), found, limit=4 << 20,
    )
    return remainder, coefficients, projections


def solution(mesh):
    in_specs = (
        P(None, "slab", "block", None),
        P(None, "slab", "block", None),
        P(),
        P(None, None, "slab", "block", None),
        P("slab", "block", None),
        P("slab", "block", None),
        P(),
        P(("slab", "block"), None),
    )
    out_specs = (P(None, "slab", "block", None), P(), P())
    return jax.shard_map(shards, mesh=mesh, in_specs=in_specs, out_specs=out_specs, check_vma=False)
```

```python
import functools

import jax
import jax.numpy as jnp
from jax import lax
from jax.experimental import pallas as pl
from jax.experimental.pallas import tpu as pltpu
from jax.sharding import PartitionSpec as P


BRICK = 8
ITERS = 3
SHIFT_MASS = 0.02
SMOOTH_WEIGHT = 0.5
VOID_DENSITY = 0.1

AXES = ("slab", "block")
LANES = 128
WIDE = (8, 24)
MID = (4, 16)
OWN = (0, 8)
REACH = 2 * ITERS
HALF = [(-1, -1), (-1, 0), (-1, 1), (0, -1)]
f32 = jnp.float32


def along_z(chunks, dz):
    lane = lax.broadcasted_iota(jnp.int32, chunks[0].shape, 1)
    turned = [pltpu.roll(chunk, (-dz) % LANES, 1) for chunk in chunks]
    edge = 0 if dz < 0 else LANES - 1
    out = []
    for number, chunk in enumerate(turned):
        other = number + dz
        filler = turned[other] if 0 <= other < len(turned) else 0.0
        out.append(jnp.where(lane == edge, filler, chunk))
    return out


def shift_store(dest, at, fields, source, target):
    src_off, src_rows = source
    dst_off, dst_rows = target
    for comp, field in enumerate(fields):
        for dy in (-1, 0, 1):
            shift = src_off - dst_off + dy
            moved = field if shift == 0 else pltpu.roll(field, (-shift) % src_rows, 0)
            if dst_rows != src_rows:
                moved = moved[:dst_rows]
            dest[(dy + 1) * len(fields) + comp, at] = moved


def gather_z(parts):
    flat, up, down = zip(*parts)
    above, below = along_z(up, 1), along_z(down, -1)
    return jnp.concatenate([a + (b + c) for a, b, c in zip(flat, above, below)], axis=1)


def stencil(moved, at, coup, center):
    depth = moved.shape[3]
    parts = [[], [], []]
    rows = []
    for low in range(0, depth, LANES):
        cut = slice(low, low + LANES)
        near = [moved[3 + c, at, :, cut] for c in range(3)]
        rows.append(near)
        flat, up, down = [], [], [None] * 6
        for i, value in enumerate(six_of(near)):
            flat.append(center(i, cut) * value)
            up.append(coup[18 * len(HALF) + i] * value)
        for q, (dx, dy) in enumerate(HALF):
            plus = [moved[(dy + 1) * 3 + c, at + dx, :, cut] for c in range(3)]
            minus = [moved[(1 - dy) * 3 + c, at - dx, :, cut] for c in range(3)]
            for i, value in enumerate(six_of([p + m for p, m in zip(plus, minus)])):
                flat[i] = flat[i] + coup[q * 18 + i] * value
                up[i] = up[i] + coup[q * 18 + 6 + i] * value
            for i, value in enumerate(six_of([p - m for p, m in zip(plus, minus)])):
                term = coup[q * 18 + 12 + i] * value
                down[i] = term if down[i] is None else down[i] + term
        flat, up, down = fold(flat), fold(up), fold(down)
        for k in range(3):
            parts[k].append((flat[k], up[k] + down[k], up[k] - down[k]))
    near = [jnp.concatenate([row[k] for row in rows], axis=1) for k in range(3)]
    return [gather_z(one) for one in parts], near


def fold(six):
    return [six[0] + (six[3] + six[4]), six[1] + (six[3] + six[5]), six[2] + (six[4] + six[5])]


def six_of(three):
    return [*three, three[0] + three[1], three[0] + three[2], three[1] + three[2]]


def loop(low, high, body):
    def step(i, carry):
        body(i)
        return carry

    lax.fori_loop(low, high, step, 0)


def row_sum(x):
    return jnp.sum(x, axis=0, keepdims=True)


def to_lanes(rows):
    column = jnp.sum(rows, axis=1, keepdims=True)
    count = rows.shape[0]
    here = lax.broadcasted_iota(jnp.int32, (count, LANES), 0)
    lane = lax.broadcasted_iota(jnp.int32, (count, LANES), 1)
    return row_sum(jnp.where(here == lane, column, 0.0))


def pick(row, index):
    lane = lax.broadcasted_iota(jnp.int32, row.shape, 1)
    return jnp.sum(jnp.where(lane == index, row, 0.0), axis=1, keepdims=True)


def scalar(one):
    return one[0, 0]


def coarse_values(means, rows, store):
    shape = (means.shape[0], rows.shape[1])
    row = lax.broadcasted_iota(jnp.int32, shape, 0)
    lane = lax.broadcasted_iota(jnp.int32, shape, 1)
    spread = jnp.zeros(shape, f32)
    for k in range(3):
        spread = jnp.where(lane == 3 * row + k, means[:, k : k + 1], spread)
    column = jnp.sum(rows[...] * row_sum(spread), axis=1, keepdims=True)
    for slot in range(27):
        store[slot] = column[slot, 0]


def correction(store, x, k, layout, span, depth):
    off, rows = layout
    base = lax.div(x + span, span) * 9 + k
    row = lax.broadcasted_iota(jnp.int32, (rows, depth), 0)
    high = jnp.where(row < off + 8, store[base + 3], store[base + 6])
    return jnp.where(row < off, store[base], high)


def send(msg, low, row, count):
    width = row.shape[1]
    msg[:, :, low : low + width] = jnp.broadcast_to(row.reshape(1, 1, width), (count, 1, width))


def pack_kernel(
    dims, where, occupancy, vector_in, young_in, cinv_in,
    near, far, vector, stiff, coarse,
    young, cinv, sems,
):
    span, depth, _ = dims
    copies = [
        pltpu.make_async_copy(source, target, sems.at[number])
        for number, (source, target) in enumerate([(young_in, young), (cinv_in, cinv), (vector_in, vector)])
    ]
    for copy in copies:
        copy.start()
    lane = lax.broadcasted_iota(jnp.int32, (8, depth), 1)
    density = jnp.full((8, depth), VOID_DENSITY, f32)
    for brick in range(depth // BRICK):
        solid = jnp.where(occupancy[brick] == 1, 1.0, VOID_DENSITY).astype(f32)
        density = jnp.where(lane // BRICK == brick, solid, density)
    for copy in copies:
        copy.wait()
    for x in range(span):
        stiff[x] = density * young[x]
    width = cinv.shape[1]
    coarse[...] = jnp.zeros_like(coarse)
    for t in range(coarse.shape[0]):
        count = min(depth, width - t * depth)
        coarse[t, 0:3, 0:count] = cinv[:, t * depth : t * depth + count]
    flip = where[0] % 2 == 1
    halo = REACH + 1

    def put(tile, low, high):
        near[tile] = jnp.where(flip, low, high)
        far[tile] = jnp.where(flip, high, low)

    for k in range(3):
        for j in range(REACH):
            put(k * REACH + j, vector[k, j], vector[k, span - REACH + j])
    for j in range(halo):
        put(3 * REACH + j, stiff[j], stiff[span - halo + j])
    for t in range(coarse.shape[0]):
        put(3 * REACH + halo + t, coarse[t], coarse[t])


def tall_kernel(dims, where, near, far, vector, stiff, coarse, tall, tall_v):
    span, _, _ = dims
    halo = REACH + 1
    flip = where[0] % 2 == 1

    def sides(tile):
        first, second = near[tile], far[tile]
        return jnp.where(flip, first, second), jnp.where(flip, second, first)

    for k in range(3):
        base = k * (span + 2 * REACH)
        for j in range(REACH):
            tall_v[base + j], tall_v[base + REACH + span + j] = sides(k * REACH + j)
        for x in range(span):
            tall_v[base + REACH + x] = vector[k, x]
    base = 0
    for j in range(halo):
        tall[base + j], tall[base + halo + span + j] = sides(3 * REACH + j)
    for x in range(span):
        tall[base + halo + x] = stiff[x]
    base, pieces = base + span + 2 * halo, coarse.shape[0]
    for t in range(pieces):
        tall[base + t], tall[base + 2 * pieces + t] = sides(3 * REACH + halo + t)
        tall[base + pieces + t] = coarse[t]


def side_tiles(where, even, odd, mid):
    flip = where[1] % 2 == 1

    def three(tile):
        first, second = even[tile], odd[tile]
        return jnp.where(flip, first, second), mid[tile], jnp.where(flip, second, first)

    return three


def repack(field):
    return pltpu.roll(field, WIDE[1] - (WIDE[0] - MID[0]), 0)[: MID[1]]


def own_of(field):
    return pltpu.roll(field, MID[1] - MID[0], 0)[:8]


def center_row(moved_root, at, root, coup):
    depth = root.shape[1]
    parts = [[] for _ in range(6)]
    for low in range(0, depth, LANES):
        cut = slice(low, low + LANES)
        flat, down = [None] * 6, [None] * 6
        near = moved_root[1, at, :, cut]
        up = [coup[18 * len(HALF) + i] * near for i in range(6)]
        for q, (dx, dy) in enumerate(HALF):
            plus, minus = moved_root[dy + 1, at + dx, :, cut], moved_root[1 - dy, at - dx, :, cut]
            both, change = plus + minus, plus - minus
            for i in range(6):
                first, last = coup[q * 18 + i] * both, coup[q * 18 + 12 + i] * change
                flat[i] = first if flat[i] is None else flat[i] + first
                up[i] = up[i] + coup[q * 18 + 6 + i] * both
                down[i] = last if down[i] is None else down[i] + last
        for i in range(6):
            parts[i].append((flat[i], up[i] + down[i], up[i] - down[i]))
    total = [gather_z(one) for one in parts]
    inside = root > 0.0
    inverse = jnp.where(inside, 1.0 / jnp.where(inside, root, 1.0), 0.0)
    center = [-total[i] * inverse for i in range(6)]
    center[:3] = [one + SHIFT_MASS for one in center[:3]]
    whole = fold(center)
    half = [jnp.where(inside, SMOOTH_WEIGHT / one, 0.0) for one in whole]
    return center, half, inverse


def setup_kernel(
    dims, where, coup, even, odd, mid,
    kh_w, h_w, inverse_w, root_w, kh_m, h_m, root_m, kh_o, root_o, coarse_rows,
    moved_root, root_all,
):
    span, depth, _ = dims
    halo = REACH + 1
    three = side_tiles(where, even, odd, mid)

    def wide(tile):
        return jnp.concatenate(three(tile), axis=0)


    def roots(x):
        root = jnp.sqrt(wide(x))
        root_all[x] = root
        shift_store(moved_root, x, [root], WIDE, WIDE)

    def diagonals(x, also_mid, also_own):
        at = x + 1
        root = root_all[at]
        center, half, inverse = center_row(moved_root, at, root, coup)
        m, o = x - (REACH - 4), x - REACH
        root_w[x] = root
        inverse_w[x] = inverse
        for k in range(3):
            h_w[k, x] = half[k]
        for i in range(6):
            kh_w[i, x] = center[i]
        if also_mid:
            root_m[m] = repack(root)
            for k in range(3):
                h_m[k, m] = repack(half[k])
            for i in range(6):
                kh_m[i, m] = repack(center[i])
        if also_own:
            own = slice(WIDE[0], WIDE[0] + 8)
            root_o[o] = root[own]
            for i in range(6):
                kh_o[i, o] = center[i][own]

    loop(0, span + 2 * halo, roots)

    def both(also_mid, also_own):
        def body(x):
            diagonals(x, also_mid, also_own)

        return body

    edge = REACH - 4
    loop(0, edge, both(False, False))
    loop(edge, REACH, both(True, False))
    loop(REACH, REACH + span, both(True, True))
    loop(REACH + span, edge + span + 8, both(True, False))
    loop(edge + span + 8, span + 2 * REACH, both(False, False))

    base = span + 2 * halo
    pieces = coarse_rows.shape[1] // depth
    coarse_rows[...] = jnp.zeros_like(coarse_rows)
    for bx in range(3):
        for t in range(pieces):
            for by, tile in enumerate(three(base + bx * pieces + t)):
                low = (bx * 3 + by) * 3
                coarse_rows[low : low + 3, t * depth : (t + 1) * depth] = tile[:3]


def vector_kernel(
    dims, where, coup, even, odd, mid, h_w, inverse_w, kh_o, root_o,
    v_w, v_m, v_o, msg,
    moved_own, sums,
):
    span, depth, devices = dims
    three = side_tiles(where, even, odd, mid)
    count = span + 2 * REACH

    def take(also_mid, also_own):
        def body(x):
            for k in range(3):
                vector = jnp.concatenate(three(k * count + x), axis=0) * inverse_w[x]
                v_w[k, x] = vector
                if also_mid:
                    v_m[k, x - (REACH - 4)] = repack(vector)
                if also_own:
                    v_o[k, x - REACH] = vector[WIDE[0] : WIDE[0] + 8]

        return body

    edge = REACH - 4
    loop(0, edge, take(False, False))
    loop(edge, REACH, take(True, False))
    loop(REACH, REACH + span, take(True, True))
    loop(REACH + span, edge + span + 8, take(True, False))
    loop(edge + span + 8, count, take(False, False))

    def smooth(x):
        at = x + REACH - 1
        shift_store(moved_own, x, [h_w[k, at] * v_w[k, at] for k in range(3)], WIDE, OWN)

    loop(0, span + 2, smooth)

    def remain(x, carry):
        for i in (2 * x, 2 * x + 1):
            image, _ = stencil(moved_own, i + 1, coup, lambda slot, cut: kh_o[slot, i, :, cut])
            carry = tuple(carry[k] + root_o[i] * (v_o[k, i] - image[k]) for k in range(3))
        return carry

    zero = jnp.zeros((8, depth), f32)
    parts = lax.fori_loop(0, span // 2, remain, (zero, zero, zero))
    sums[...] = jnp.zeros_like(sums)
    for k in range(3):
        sums[k : k + 1] = row_sum(parts[k])
    send(msg, 0, to_lanes(sums[...]) * (1.0 / (span * 8 * depth)), devices)


def iterate(dims, level, layouts, coup, store, residual, half, root, center, moved, moved_next, z_all, image):
    span, depth = dims
    source, first, second = layouts

    def begin(x):
        fields = []
        for k in range(3):
            fix = correction(store, x - level, k, source, span, depth)
            fields.append(half(k, x) * residual(k, x) + root(x) * fix)
        shift_store(moved, x, fields, source, first)

    def middle(x):
        at = x + 1
        out, near = stencil(moved, at, coup, center(at))
        fields = [near[k] + half(k, at) * (residual(k, at) - out[k]) for k in range(3)]
        for k in range(3):
            z_all[k, x] = fields[k]
        shift_store(moved_next, x, fields, first, second)

    loop(0, span + 2 * level, begin)
    loop(0, span + 2 * level - 2, middle)
    if image is not None:
        loop(0, span + 2 * level - 4, image)


def own_rows(layout):
    return slice(layout[0], layout[0] + 8)


def means_of(dims, coup, root, half, mapped, center, moved_own):
    span, depth = dims

    def begin(x):
        shift_store(moved_own, x, [half(k, x) * mapped(k, x) for k in range(3)], MID, OWN)

    def body(x, carry):
        for i in (2 * x, 2 * x + 1):
            image, _ = stencil(moved_own, i + 1, coup, lambda slot, cut: center(slot, i, cut))
            carry = tuple(carry[k] + root(i) * (own_of(mapped(k, i + 1)) - image[k]) for k in range(3))
        return carry

    loop(0, span + 2, begin)
    zero = jnp.zeros((8, depth), f32)
    return lax.fori_loop(0, span // 2, body, (zero, zero, zero))


def first_kernel(
    dims, coup, got, coarse_rows, kh_w, h_w, v_w, root_w, kh_m, h_m, kh_o, v_o, root_o,
    z_own, mapped, msg,
    moved, moved_next, moved_own, z_all, store, sums,
):
    span, depth, devices = dims
    level = REACH
    coarse_values(got[:, 0], coarse_rows, store)

    def image(x):
        out, _ = stencil(moved_next, x + 1, coup, lambda i, cut: kh_m[i, x, :, cut])
        for k in range(3):
            mapped[k, x] = out[k]

    iterate(
        (span, depth), level, (WIDE, WIDE, MID), coup, store,
        lambda k, x: v_w[k, x], lambda k, x: h_w[k, x], lambda x: root_w[x],
        (lambda at: lambda i, cut: kh_w[i, at, :, cut]), moved, moved_next, z_all, image,
    )
    inner = level - 2
    parts = means_of(
        (span, depth), coup, lambda x: root_o[x],
        lambda k, x: h_m[k, x + 3], lambda k, x: mapped[k, x + inner - 1],
        lambda i, x, cut: kh_o[i, x, :, cut], moved_own,
    )

    def dots(x, carry):
        gamma, delta = carry
        for k in range(3):
            z = z_all[k, x + level - 1, own_rows(WIDE)]
            z_own[k, x] = z
            gamma = gamma + v_o[k, x] * z
            delta = delta + own_of(mapped[k, x + inner]) * z
        return gamma, delta

    zero = jnp.zeros((8, depth), f32)
    gamma, delta = lax.fori_loop(0, span, dots, (zero, zero))
    scale = 1.0 / (span * 8 * depth)
    sums[...] = jnp.zeros_like(sums)
    for k in range(3):
        sums[k : k + 1] = row_sum(parts[k]) * scale
    sums[3:4] = row_sum(gamma)
    sums[4:5] = row_sum(delta)
    send(msg, 0, to_lanes(sums[...]), devices)


def second_kernel(
    dims, coup, got, first, coarse_rows, kh_m, h_m, v_m, root_m, kh_o, root_o, mapped_old,
    z_own, mapped, residual, means, msg,
    moved, moved_next, moved_own, z_all, store, sums,
):
    span, depth, devices = dims
    level = REACH - 2
    total = row_sum(got[:, 0])
    gamma = pick(total, 3)
    step = gamma / pick(total, 4)
    fresh = first[:, 0] - step * got[:, 0]
    means[...] = fresh
    coarse_values(fresh, coarse_rows, store)
    size = scalar(step)

    def rest(k, x):
        return v_m[k, x] - size * mapped_old[k, x]

    def image(x):
        out, _ = stencil(moved_next, x + 1, coup, lambda i, cut: kh_m[i, x + 2, :, cut])
        for k in range(3):
            mapped[k, x] = out[k]

    iterate(
        (span, depth), level, (MID, MID, MID), coup, store,
        rest, lambda k, x: h_m[k, x], lambda x: root_m[x],
        (lambda at: lambda i, cut: kh_m[i, at, :, cut]), moved, moved_next, z_all, image,
    )
    inner = level - 2
    parts = means_of(
        (span, depth), coup, lambda x: root_o[x],
        lambda k, x: h_m[k, x + 3], lambda k, x: mapped[k, x + inner - 1],
        lambda i, x, cut: kh_o[i, x, :, cut], moved_own,
    )

    def dots(x, carry):
        gamma, delta, cross = carry
        for k in range(3):
            z = own_of(z_all[k, x + level - 1])
            z_own[k, x] = z
            gamma = gamma + own_of(rest(k, x + level)) * z
            delta = delta + own_of(mapped[k, x + inner]) * z
            cross = cross + own_of(mapped_old[k, x + 4]) * z
        return gamma, delta, cross

    zero = jnp.zeros((8, depth), f32)
    dotted = lax.fori_loop(0, span, dots, (zero, zero, zero))

    def keep(x):
        for k in range(3):
            residual[k, x] = rest(k, x + inner)

    loop(0, span + 2 * inner, keep)
    scale = 1.0 / (span * 8 * depth)
    sums[...] = jnp.zeros_like(sums)
    for k in range(3):
        sums[k : k + 1] = row_sum(parts[k]) * scale
        sums[k + 3 : k + 4] = row_sum(dotted[k])
    send(msg, 0, to_lanes(sums[...]), devices)


def third_kernel(
    dims, coup, got, got_old, means, coarse_rows, kh_m, h_m, root_m, kh_o, v_o, root_o,
    z_old, mapped_old, z_new, mapped_new, residual_old, lanczos, previous, locked,
    base, z_out, dir_out, scal, msg,
    moved, moved_next, residual, mapped, z_all, store, sums, locked_sums,
):
    span, depth, devices = dims
    level = REACH - 4
    total_old = row_sum(got_old[:, 0])
    total = row_sum(got[:, 0])
    gamma_old = pick(total_old, 3)
    delta_old = pick(total_old, 4)
    step_old = gamma_old / delta_old
    gamma = pick(total, 3)
    ratio = gamma / gamma_old
    delta = pick(total, 4) + 2.0 * ratio * pick(total, 5) + ratio * ratio * delta_old
    step = gamma / delta
    fresh = means[...] - step * (got[:, 0] + ratio * got_old[:, 0])
    coarse_values(fresh, coarse_rows, store)
    lane = lax.broadcasted_iota(jnp.int32, (1, LANES), 1)
    scal[...] = jnp.where(lane == 0, gamma, jnp.where(lane == 1, delta, 0.0))
    size, size_old, blend = scalar(step), scalar(step_old), scalar(ratio)

    def update(x):
        for k in range(3):
            mapped[k, x] = mapped_new[k, x] + blend * mapped_old[k, x + 2]
            residual[k, x] = residual_old[k, x] - size * mapped[k, x]

    loop(0, span + 2 * level, update)
    iterate(
        (span, depth), level, (MID, MID, OWN), coup, store,
        lambda k, x: residual[k, x], lambda k, x: h_m[k, x + 2], lambda x: root_m[x + 2],
        (lambda at: lambda i, cut: kh_m[i, at + 2, :, cut]), moved, moved_next, z_all, None,
    )

    def finish(x, carry):
        gamma, delta, cross, with_base, with_z, with_dir, weight = carry
        image, near = stencil(moved_next, x + 1, coup, lambda i, cut: kh_o[i, x, :, cut])
        inverse = 1.0 / root_o[x]
        for k in range(3):
            z = near[k]
            direction = z_new[k, x] + blend * z_old[k, x]
            partial = size_old * z_old[k, x] + size * direction
            vector = v_o[k, x]
            gamma = gamma + own_of(residual[k, x + level]) * z
            delta = delta + image[k] * z
            cross = cross + own_of(mapped[k, x + level]) * z
            with_base = with_base + vector * partial
            with_z = with_z + vector * z
            with_dir = with_dir + vector * direction
            weight = weight + lanczos[k, x] * lanczos[k, x]
            z_out[k, x] = z * inverse
            dir_out[k, x] = direction * inverse
            base[k, x] = partial * inverse - coup[18 * len(HALF) + 6] * previous[k, x]
        return gamma, delta, cross, with_base, with_z, with_dir, weight

    zero = jnp.zeros((8, depth), f32)
    dotted = lax.fori_loop(0, span // 2, lambda x, carry: finish(2 * x + 1, finish(2 * x, carry)), (zero,) * 7)
    sums[...] = jnp.zeros_like(sums)
    for k in range(7):
        sums[k : k + 1] = row_sum(dotted[k])

    def project(n):
        def body(x, carry):
            out = list(carry)
            for k in range(3):
                vector = locked[n, k, x]
                out[0] = out[0] + vector * base[k, x]
                out[1] = out[1] + vector * z_out[k, x]
                out[2] = out[2] + vector * dir_out[k, x]
                out[3] = out[3] + vector * lanczos[k, x]
            return tuple(out)

        four = lax.fori_loop(0, span, body, (zero,) * 4, unroll=True)
        rows = [row_sum(one) for one in four]
        locked_sums[n] = jnp.concatenate(rows, axis=0)

    count = locked.shape[0]
    loop(0, count, project)
    send(msg, 0, to_lanes(sums[...]), devices)
    flat = locked_sums[...].reshape(count * 4, depth)
    send(msg, LANES, to_lanes(flat), devices)


def last_kernel(
    dims, got, scal, base, z, direction, lanczos, locked,
    remainder, weights, found, msg,
    sums,
):
    span, depth, devices = dims
    count = locked.shape[0]
    total = row_sum(got[:, 0])
    head, tail = total[:, :LANES], total[:, LANES:]
    gamma_old, delta_old = pick(scal[...], 0), pick(scal[...], 1)
    gamma = pick(head, 0)
    ratio = gamma / gamma_old
    delta = pick(head, 1) + 2.0 * ratio * pick(head, 2) + ratio * ratio * delta_old
    step = gamma / delta
    inner = pick(head, 3) + step * (pick(head, 4) + ratio * pick(head, 5))
    alpha = inner / pick(head, 6)
    lane = lax.broadcasted_iota(jnp.int32, (1, LANES), 1)
    kind = lane % 4
    factor = jnp.where(kind == 0, 1.0, jnp.where(kind == 1, step, jnp.where(kind == 2, step * ratio, -alpha)))
    terms = jnp.where(lane < 4 * count, tail * factor, 0.0)
    for n in range(count):
        value = jnp.sum(jnp.where(lane // 4 == n, terms, 0.0), axis=1, keepdims=True)
        weights[n] = scalar(value)
    found[0] = scalar(alpha)
    size, both, shrink = scalar(step), scalar(step * ratio), scalar(alpha)

    def body(x, square):
        for k in range(3):
            rest = base[k, x] + size * z[k, x] + both * direction[k, x] - shrink * lanczos[k, x]
            taken = weights[0] * locked[0, k, x]
            for n in range(1, count):
                taken = taken + weights[n] * locked[n, k, x]
            rest = rest - taken
            remainder[k, x] = rest
            square = square + rest * rest
        return square

    square = lax.fori_loop(0, span, body, jnp.zeros((8, depth), f32))
    sums[...] = jnp.zeros_like(sums)
    sums[0:1] = row_sum(square)
    send(msg, 0, to_lanes(sums[...]), devices)


def closing_kernel(cells, got, found, out):
    total = jnp.sum(row_sum(got[:, 0])[:, :8], axis=1, keepdims=True)
    out[0] = found[0]
    out[1] = scalar(jnp.sqrt(total / cells))


VMEM = pl.BlockSpec(memory_space=pltpu.VMEM)
SMEM = pl.BlockSpec(memory_space=pltpu.SMEM)
HBM = pl.BlockSpec(memory_space=pltpu.HBM)


def call(kernel, outs, scratch, *operands, limit, stay=0):
    places = [SMEM if len(operand.shape) == 1 else VMEM for operand in operands]
    if stay:
        places[-stay:] = [HBM] * stay
        kept = [pltpu.with_memory_space_constraint(operand, pltpu.HBM) for operand in operands[-stay:]]
        operands = (*operands[:-stay], *kept)
    return pl.pallas_call(
        kernel,
        out_shape=[jax.ShapeDtypeStruct(shape, f32) for shape in outs],
        in_specs=places,
        out_specs=[SMEM if len(shape) == 1 else VMEM for shape in outs],
        scratch_shapes=scratch,
        compiler_params=pltpu.CompilerParams(vmem_limit_bytes=limit),
    )(*operands)


def swap_permutes(axis):
    count = lax.axis_size(axis)
    near = [(i, i ^ 1) for i in range(count) if i ^ 1 < count]
    far = [(i, ((i + 1) ^ 1) - 1) for i in range(count)]
    return near, [(i, j) for i, j in far if 0 <= j < count]


def exchange_rows(rows):
    return lax.all_to_all(rows, AXES, 0, 0, tiled=True)


def shards(
    lanczos_vector, previous_vector, previous_beta, locked_vectors, occupancy, young, couplings, coarse_inverse
):
    _, span, span_y, depth = lanczos_vector.shape
    counts = (lax.axis_size("slab"), lax.axis_size("block"))
    devices = counts[0] * counts[1]
    locked = locked_vectors.shape[0]
    halo = REACH + 1
    assert span_y == 8 and span >= halo and locked * 4 <= LANES
    slab, block = lax.axis_index("slab"), lax.axis_index("block")
    where = jnp.stack([slab, block]).astype(jnp.int32)
    flat = -couplings.reshape(-1, 9)
    a, b, c = flat[:, 1], flat[:, 2], flat[:, 5]
    six = jnp.stack([flat[:, 0] - a - b, flat[:, 4] - a - c, flat[:, 8] - b - c, a, b, c], axis=1)
    flat, up, down = six[1:12:3], six[2:12:3], six[0:12:3]
    groups = jnp.stack([flat, 0.5 * (up + down), 0.5 * (up - down)], axis=1)
    coup = jnp.concatenate([groups.reshape(-1), six[12], previous_beta.reshape(1)])

    dims = (span, depth, devices)
    pieces = -(-coarse_inverse.shape[1] // depth)
    own = (3, span, 8, depth)

    def scratch(*shape):
        return pltpu.VMEM(shape, f32)

    tiles = (3 * REACH + halo + pieces, 8, depth)
    near, far, vector, stiff, coarse = call(
        functools.partial(pack_kernel, dims),
        [tiles, tiles, own, own[1:], (pieces, 8, depth)],
        [scratch(*own[1:]), scratch(*coarse_inverse.shape), pltpu.SemaphoreType.DMA((3,))],
        where, pltpu.with_memory_space_constraint(occupancy.reshape(-1), pltpu.HBM), lanczos_vector, young, coarse_inverse, limit=6 << 20, stay=3,
    )
    to_near, to_far = swap_permutes("slab")
    near, far = lax.ppermute(near, "slab", to_near), lax.ppermute(far, "slab", to_far)
    tall, tall_v = call(
        functools.partial(tall_kernel, dims),
        [(span + 2 * halo + 3 * pieces, 8, depth), (3 * (span + 2 * REACH), 8, depth)],
        [],
        where, near, far, vector, stiff, coarse, limit=6 << 20,
    )
    to_near, to_far = swap_permutes("block")
    tall, tall_v, coup = lax.optimization_barrier((tall, tall_v, coup))
    side_near = lax.ppermute(tall, "block", to_near)
    side_far = lax.ppermute(tall, "block", to_far)
    near_v = lax.ppermute(tall_v, "block", to_near)
    far_v = lax.ppermute(tall_v, "block", to_far)

    wide = (span + 2 * REACH, WIDE[1], depth)
    mid = (span + 8, MID[1], depth)
    row = (devices, 1, LANES)
    kh_w, h_w, inverse_w, root_w, kh_m, h_m, root_m, kh_o, root_o, rows = call(
        functools.partial(setup_kernel, dims),
        [
            (6, *wide), (3, *wide), wide, wide, (6, *mid), (3, *mid), mid,
            (6, *own[1:]), own[1:], (32, pieces * depth),
        ],
        [scratch(3, span + 2 * halo, WIDE[1], depth), scratch(span + 2 * halo, WIDE[1], depth)],
        where, coup, side_near, side_far, tall, limit=9 << 20,
    )
    v_w, v_m, v_o, msg = call(
        functools.partial(vector_kernel, dims),
        [(3, *wide), (3, *mid), own, row],
        [scratch(9, span + 2, 8, depth), scratch(8, depth)],
        where, coup, near_v, far_v, tall_v, h_w, inverse_w, kh_o, root_o, limit=9 << 20,
    )
    first = exchange_rows(msg)

    store = pltpu.SMEM((27,), f32)
    z_0, mapped_0, msg = call(
        functools.partial(first_kernel, dims),
        [own, (3, *mid), row],
        [
            scratch(9, *wide),
            scratch(9, span + 2 * REACH - 2, MID[1], depth),
            scratch(9, span + 2, 8, depth),
            scratch(3, span + 2 * REACH - 2, WIDE[1], depth),
            store,
            scratch(8, depth),
        ],
        coup, first, rows, kh_w, h_w, v_w, root_w, kh_m, h_m, kh_o, v_o, root_o, limit=14 << 20,
    )
    got_0 = exchange_rows(msg)

    level = REACH - 2
    inner = (3, span + 2 * level - 4, MID[1], depth)
    z_1, mapped_1, residual, means, msg = call(
        functools.partial(second_kernel, dims),
        [own, inner, inner, (devices, LANES), row],
        [
            scratch(9, *mid),
            scratch(9, span + 2 * level - 2, MID[1], depth),
            scratch(9, span + 2, 8, depth),
            scratch(3, span + 2 * level - 2, MID[1], depth),
            store,
            scratch(8, depth),
        ],
        coup, got_0, first, rows, kh_m, h_m, v_m, root_m, kh_o, root_o, mapped_0, limit=10 << 20,
    )
    got_1 = exchange_rows(msg)

    level = REACH - 4
    base, z_2, direction, scal, msg = call(
        functools.partial(third_kernel, dims),
        [own, own, own, (1, LANES), (devices, 1, 2 * LANES)],
        [
            scratch(9, span + 2 * level, MID[1], depth),
            scratch(9, span + 2 * level - 2, 8, depth),
            scratch(3, span + 2 * level, MID[1], depth),
            scratch(3, span + 2 * level, MID[1], depth),
            scratch(3, span + 2 * level - 2, MID[1], depth),
            store,
            scratch(8, depth),
            scratch(locked, 4, depth),
        ],
        coup, got_1, got_0, means, rows, kh_m, h_m, root_m, kh_o, v_o, root_o,
        z_0, mapped_0, z_1, mapped_1, residual, lanczos_vector, previous_vector, locked_vectors, limit=9 << 20,
    )
    got_2 = exchange_rows(msg)

    remainder, projections, found, msg = call(
        functools.partial(last_kernel, dims),
        [own, (locked,), (1,), row],
        [scratch(8, depth)],
        got_2, scal, base, z_2, direction, lanczos_vector, locked_vectors, limit=6 << 20,
    )
    (coefficients,) = call(
        functools.partial(closing_kernel, 3.0 * span * span_y * depth * devices),
        [(2,)],
        [],
        exchange_rows(msg), found, limit=4 << 20,
    )
    return remainder, coefficients, projections


def solution(mesh):
    in_specs = (
        P(None, "slab", "block", None),
        P(None, "slab", "block", None),
        P(),
        P(None, None, "slab", "block", None),
        P("slab", "block", None),
        P("slab", "block", None),
        P(),
        P(("slab", "block"), None),
    )
    out_specs = (P(None, "slab", "block", None), P(), P())
    return jax.shard_map(shards, mesh=mesh, in_specs=in_specs, out_specs=out_specs, check_vma=False)
```
